256 devices in a mesh: view: 32 (over z, y_lo, core), head: 8 (over x, y_hi).
Axes of the slice: x: 4, y: 4 (y_hi: 2, y_lo: 2; y = y_hi * 2 + y_lo), z: 8, core: 2. Of those that a mesh axis runs over, the one named last changes fastest.
Arguments:
- tokens: bfloat16 [8192, 1536], P('view'), may hold values from -8 to 8
- timesteps: int32 [128], P('view'), may hold values from 0 to 999
- adjacency: int32 [128, 6], P('view'), may hold values from 0 to 127, as said below
- neighbour_count: int32 [128], P('view'), may hold values from 2 to 6, as said below
- anchor: int32 [1], replicated, may hold values from 0 to 127
- mod_weight: bfloat16 [256, 6, 1536], P(None, None, 'head'), may hold values from -1.5 to 1.5
- qkv_weight: bfloat16 [1536, 3, 1536], P(None, None, 'head'), may hold values from -1 to 1
- qk_gain: float32 [2, 1536], P(None, 'head'), may hold values from 0.6 to 7.2
- out_weight: bfloat16 [1536, 1536], P('head'), may hold values from -0.15625 to 0.15625
- up_weight: bfloat16 [1536, 6144], P(None, 'head'), may hold values from -0.15625 to 0.15625
- down_weight: bfloat16 [6144, 1536], P('head'), may hold values from -0.078125 to 0.078125
Outputs:
- output: bfloat16 [8192, 1536], P('view')
The draws below stay inside these ranges and needn't reach their ends.
Inputs may be any that keep to these rules, and one draw needn't show every extreme that they name: `adjacency`: views lie on a closed camera orbit of 128 views (view 128 - 1 beside view 0). Row v names 6 different views other than v, each at most 8 views from v along the orbit; in every draw some used neighbour is exactly 8 views away on each side. Only the first neighbour_count[v] entries are used. `neighbour_count`: some view has 6 neighbours and some view has 2 in every draw.
All inputs are finite; a program needn't handle non-finite values.
Results may differ from the reference program's by a relative error of at most 0.025.
Values may be sent and summed in bfloat16 or wider, within the bound.
A program may use at most 128 MiB of HBM per device.

```python
import math
import jax
import jax.numpy as jnp
from jax import lax

HEADS = 24
HD = 64
FF = 6144
TFREQ = 256
TOK = 64
MAXNB = 6
D = 1536
RADIUS = 8
VIEWS = 128
N_HEAD = 8


def neighbour_lists(key):
    row_keys = jax.random.split(jax.random.fold_in(key, 101), VIEWS)
    ranks = jax.vmap(lambda row_key: jax.random.permutation(row_key, 2 * RADIUS))(row_keys).astype(jnp.int32)
    offsets = jnp.where(ranks < RADIUS, ranks + 1, RADIUS - 1 - ranks)[:, :MAXNB]
    middle = jax.random.permutation(jax.random.fold_in(key, 102), 2 * RADIUS - 2).astype(jnp.int32)
    middle_offsets = jnp.where(middle < RADIUS - 1, middle + 1, RADIUS - 2 - middle)
    forced = jnp.concatenate([jnp.array([RADIUS, -RADIUS], dtype=jnp.int32), middle_offsets[:MAXNB - 2]])
    busiest = jax.random.randint(jax.random.fold_in(key, 103), (), 0, VIEWS)
    lightest = (busiest + jax.random.randint(jax.random.fold_in(key, 104), (), 1, VIEWS)) % VIEWS
    view_ids = jnp.arange(VIEWS, dtype=jnp.int32)
    offsets = jnp.where(view_ids[:, None] == busiest, forced[None, :], offsets)
    counts = jax.random.randint(jax.random.fold_in(key, 105), (VIEWS,), 2, MAXNB + 1)
    counts = jnp.where(view_ids == busiest, MAXNB, counts)
    counts = jnp.where(view_ids == lightest, 2, counts)
    adjacency = (view_ids[:, None] + offsets) % VIEWS
    return (adjacency.astype(jnp.int32), counts.astype(jnp.int32))


def draw_adjacency(key, part):
    return neighbour_lists(key)[0]


def draw_neighbour_count(key, part):
    return neighbour_lists(key)[1]


def draw_tokens(key, part):
    values = jnp.clip(jax.random.normal(jax.random.fold_in(key, 13), (VIEWS * TOK, D), jnp.float32), -6.0, 6.0)
    return values.astype(jnp.bfloat16)


def draw_qkv_weight(key, part):
    values = jax.random.normal(jax.random.fold_in(key, 22), (D, 3, D), jnp.float32) * (1.0 / math.sqrt(D))
    return jnp.clip(values, -1.0, 1.0).astype(jnp.bfloat16)


def draw_qk_gain(key, part):
    head_scale = jnp.exp(jax.random.uniform(jax.random.fold_in(key, 32), (2, HEADS), jnp.float32, 0.0, math.log(2.5)))
    channel = jax.random.uniform(jax.random.fold_in(key, 33), (2, HEADS, HD), jnp.float32, 0.9, 1.1)
    return (head_scale[:, :, None] * channel).reshape(2, D)


def set_ends(entries, key, low, high):
    index_at = [jax.random.randint(jax.random.fold_in(key, axis), (), 0, length) for axis, length in enumerate(entries.shape)]
    widest = entries.shape.index(max(entries.shape))
    neighbour = index_at[:widest] + [(index_at[widest] + 1) % entries.shape[widest]] + index_at[widest + 1:]
    return entries.at[tuple(index_at)].set(low).at[tuple(neighbour)].set(high)


def block_levels(key, dims, shards, least, top_value):
    level = 1.0
    for position, shards_of in shards:
        heights = jax.random.uniform(jax.random.fold_in(jax.random.fold_in(key, 6), position), (shards_of,), jnp.float32, least / len(shards), top_value / len(shards))
        level = level * jnp.repeat(jnp.exp(heights), dims[position] // shards_of).reshape((-1,) + (1,) * (len(dims) - 1 - position))
    return level


def centred(rng, extent, spread, limit, cuts=(), kind=jnp.bfloat16):
    values = jax.random.normal(rng, extent, jnp.float32) * spread
    if len(cuts) > 0:
        values = block_levels(rng, extent, cuts, -0.22, 0.18) * values
    return jnp.clip(values, min=-limit, max=limit).astype(kind)


def setup_inputs(seed: int = 0) -> dict:
    key_of = jax.random.split(jax.random.key(seed), 12)
    return {
        "tokens": draw_tokens(jax.random.fold_in(key_of[11], 71), 0),
        "timesteps": set_ends(jax.random.randint(key_of[1], (VIEWS,), 0, 1000), jax.random.fold_in(key_of[1], 1), 0, 999).astype(jnp.int32),
        "adjacency": draw_adjacency(jax.random.fold_in(key_of[11], 71), 0),
        "neighbour_count": draw_neighbour_count(jax.random.fold_in(key_of[11], 71), 0),
        "anchor": jax.random.randint(key_of[4], (1,), 0, VIEWS).astype(jnp.int32),
        "mod_weight": centred(key_of[5], (TFREQ, 6, D), (TFREQ // 16) ** -0.5, 1.5, ((2, 8),)),
        "qkv_weight": draw_qkv_weight(jax.random.fold_in(key_of[11], 71), 0),
        "qk_gain": draw_qk_gain(jax.random.fold_in(key_of[11], 71), 0),
        "out_weight": centred(key_of[8], (D, D), D ** -0.5, 0.15625, ((0, 8),)),
        "up_weight": centred(key_of[9], (D, FF), D ** -0.5, 0.15625, ((1, 8),)),
        "down_weight": centred(key_of[10], (FF, D), FF ** -0.5, 0.078125, ((0, 8),)),
    }


EPSILON = 1e-06

def layer_norm(values):
    centre = values - lax.optimization_barrier(jnp.mean(values, axis=-1, keepdims=True))
    return centre * lax.rsqrt(lax.optimization_barrier(jnp.mean(centre * centre, axis=-1, keepdims=True)) + EPSILON)

def head_norm(values, qk_gains):
    return values * lax.rsqrt(lax.optimization_barrier(jnp.mean(values * values, axis=-1, keepdims=True)) + EPSILON) * qk_gains

def time_features(steps_in, freq_count):
    half_count = freq_count // 2
    frequency = jnp.exp(-math.log(10000.0) * jnp.arange(half_count, dtype=jnp.float32) / half_count)
    angles = steps_in.astype(jnp.float32)[:, None] * frequency[None, :]
    return jnp.concatenate([jnp.cos(angles), jnp.sin(angles)], axis=-1)

def reference(tokens, timesteps, adjacency, neighbour_count, anchor, mod_weight, qkv_weight, qk_gain, out_weight, up_weight, down_weight):
    model_width = tokens.shape[1]
    local_width = model_width // N_HEAD
    hidden_part = FF // N_HEAD
    features = time_features(timesteps, TFREQ)
    activated = jax.nn.silu(features).astype(jnp.bfloat16)
    modulation = jnp.einsum('vf,fsd->vsd', activated.astype(jnp.float32), mod_weight.astype(jnp.float32))
    inputs = tokens.reshape(VIEWS, TOK, model_width).astype(jnp.float32)
    normed = layer_norm(inputs) * (1.0 + modulation[:, 1][:, None]) + modulation[:, 0][:, None]
    first_in = normed.astype(jnp.bfloat16).reshape(VIEWS * TOK, model_width)
    projected = jnp.dot(first_in, qkv_weight.reshape(model_width, 3 * model_width), preferred_element_type=jnp.float32)
    projected = projected.reshape(VIEWS, TOK, 3, HEADS, HD)
    qk_gains = qk_gain.reshape(2, HEADS, HD)
    queries = head_norm(projected[:, :, 0], qk_gains[0]).astype(jnp.bfloat16)
    keys_all = head_norm(projected[:, :, 1], qk_gains[1]).astype(jnp.bfloat16)
    values_all = projected[:, :, 2].astype(jnp.bfloat16)
    out_groups = out_weight.reshape(N_HEAD, local_width, model_width).astype(jnp.float32)
    down_groups = down_weight.reshape(N_HEAD, hidden_part, model_width).astype(jnp.float32)

    def one_view(view_index):
        blocks = jnp.concatenate([view_index[None], adjacency[view_index], anchor]).astype(jnp.int32)
        keys_here = keys_all[blocks].astype(jnp.float32)
        values_here = values_all[blocks].astype(jnp.float32)
        usable = jnp.concatenate([jnp.ones((1,), dtype=bool), jnp.arange(MAXNB) < neighbour_count[view_index], jnp.ones((1,), dtype=bool)])
        scores = jnp.einsum('the,bshe->htbs', queries[view_index].astype(jnp.float32), keys_here) * (1.0 / math.sqrt(HD))
        scores = jnp.where(usable[None, None, :, None], scores, -jnp.inf)
        largest = lax.optimization_barrier(jnp.max(scores, axis=(2, 3), keepdims=True))
        powers = jnp.exp(scores - largest)
        weights = (powers / lax.optimization_barrier(jnp.sum(powers, axis=(2, 3), keepdims=True))).astype(jnp.bfloat16)
        attended = jnp.einsum('htbs,bshe->the', weights.astype(jnp.float32), values_here).astype(jnp.bfloat16)
        grouped = attended.reshape(TOK, N_HEAD, local_width).astype(jnp.float32)
        partial_attn = jnp.einsum('tgc,gcd->gtd', grouped, out_groups).astype(jnp.bfloat16)
        attn_total = lax.optimization_barrier(jnp.sum(partial_attn.astype(jnp.float32), axis=0))
        residual = inputs[view_index] + modulation[view_index, 2] * attn_total
        second_in = (layer_norm(residual) * (1.0 + modulation[view_index, 4]) + modulation[view_index, 3]).astype(jnp.bfloat16)
        hidden = jax.nn.gelu(jnp.dot(second_in, up_weight, preferred_element_type=jnp.float32), approximate=True).astype(jnp.bfloat16)
        hidden_groups = hidden.reshape(TOK, N_HEAD, hidden_part).astype(jnp.float32)
        partial_mlp = jnp.einsum('tgc,gcd->gtd', hidden_groups, down_groups).astype(jnp.bfloat16)
        mlp_total = lax.optimization_barrier(jnp.sum(partial_mlp.astype(jnp.float32), axis=0))
        return (residual + modulation[view_index, 5] * mlp_total).astype(jnp.bfloat16)
    result = lax.map(one_view, jnp.arange(VIEWS, dtype=jnp.int32))
    return result.reshape(VIEWS * TOK, model_width)
```

```python
import functools
import math

import jax
import jax.numpy as jnp
from jax import lax
from jax.experimental import pallas as pl
from jax.experimental.pallas import tpu as pltpu
from jax.sharding import PartitionSpec as P

HD = 64
RADIUS = 8
EPSILON = 1e-06
MESH = pl.DeviceIdType.MESH
F32 = jnp.float32
BF16 = jnp.bfloat16

HEADS_X = 4
HEADS_Y = 2
QUAD = 4

DELTAS = [(2, 1), (1, 1), (3, 1), (2, 0), (0, 1), (1, 0), (3, 0)]


def time_features(steps_in, freq_count):
    half_count = freq_count // 2
    frequency = jnp.exp(-math.log(10000.0) * jnp.arange(half_count, dtype=jnp.float32) / half_count)
    angles = steps_in.astype(jnp.float32)[:, None] * frequency[None, :]
    return jnp.concatenate([jnp.cos(angles), jnp.sin(angles)], axis=-1)


def dot_nt(a, b):
    return lax.dot_general(a, b, (((1,), (1,)), ((), ())), preferred_element_type=F32)


def dot_nn(a, b):
    return lax.dot_general(a, b, (((1,), (0,)), ((), ())), preferred_element_type=F32)


def layer_norm(values):
    centre = values - jnp.mean(values, axis=-1, keepdims=True)
    return centre * lax.rsqrt(jnp.mean(centre * centre, axis=-1, keepdims=True) + EPSILON)


def kernel(
    n_view,
    act_ref,
    gain_ref,
    adj_ref,
    cnt_ref,
    anc_ref,
    tok_hbm,
    modw_hbm,
    qkvw_hbm,
    outw_hbm,
    upw_hbm,
    downw_hbm,
    out_ref,
    tok,
    modw,
    wq,
    wkv,
    outw,
    upw,
    downw,
    normed,
    h1,
    modbuf,
    mods,
    qs,
    kv_own,
    cand,
    kvg,
    anc_src,
    anc_a,
    anc_b,
    anc_bsrc,
    anc_csrc,
    anc_full,
    att,
    part,
    rs1,
    resid,
    h2,
    hidden,
    part2,
    rs2,
    fin,
    ld_sem,
    mod_s,
    mod_r,
    kv_s,
    kv_r,
    aa_s,
    aa_r,
    ab_s,
    ab_r,
    ac_s,
    ac_r,
    rs1_s,
    rs1_r,
    ag1_s,
    ag1_r,
    rs2_s,
    rs2_r,
    ag2_s,
    ag2_r,
):
    v = lax.axis_index("view")
    h = lax.axis_index("head")
    xx, yh = h // HEADS_Y, h % HEADS_Y
    z, q = v // QUAD, v % QUAD
    n_z = n_view // QUAD
    n_head = HEADS_X * HEADS_Y
    width = tok.shape[1]
    rows = tok.shape[0]
    blk = rows // n_head

    def head_peer(dx, dy):
        return ((xx + dx) % HEADS_X) * HEADS_Y + (yh + dy) % HEADS_Y

    def head_dev(dx, dy):
        return (v, head_peer(dx, dy))

    def view_dev(d):
        return ((v + d + n_view) % n_view, h)

    def quad_dev(dq):
        return (z * QUAD + (q + dq) % QUAD, h)

    def z_dev(dz):
        return (((z + dz) % n_z) * QUAD + q, h)

    def rcopy(src, dst, ss, rs, dev):
        return pltpu.make_async_remote_copy(
            src_ref=src, dst_ref=dst, send_sem=ss, recv_sem=rs, device_id=dev, device_id_type=MESH
        )

    barrier = pltpu.get_barrier_semaphore()
    partners = [head_dev(dx, dy) for dx, dy in DELTAS]
    partners += [view_dev(d) for d in (1, -1, 2, -2)]
    partners += [quad_dev(dq) for dq in range(1, QUAD)]
    partners += [z_dev(dz) for dz in range(1, n_z)]
    for dev in partners:
        pl.semaphore_signal(barrier, inc=1, device_id=dev, device_id_type=MESH)

    ld_mod = pltpu.make_async_copy(modw_hbm, modw, ld_sem.at[0])
    ld_mod.start()
    ld_tok = pltpu.make_async_copy(tok_hbm, tok, ld_sem.at[1])
    ld_tok.start()
    zero = jnp.zeros((HD, width), BF16)
    ld_qkv = []
    for i in range(3):
        wq[2 * i * HD + HD : 2 * i * HD + 2 * HD, :] = zero
        outw[2 * i * HD : 2 * i * HD + HD, :] = zero
        for s, (dst, at) in enumerate(
            ((wq, 2 * i * HD), (wkv, 2 * i * HD), (wkv, 2 * i * HD + HD))
        ):
            c = pltpu.make_async_copy(
                qkvw_hbm.at[s, pl.ds(i * HD, HD), :], dst.at[pl.ds(at, HD), :], ld_sem.at[2 + 3 * i + s]
            )
            c.start()
            ld_qkv.append(c)
    ld_out = []
    for i in range(3):
        c = pltpu.make_async_copy(
            outw_hbm.at[pl.ds(i * HD, HD), :], outw.at[pl.ds(2 * i * HD + HD, HD), :], ld_sem.at[11 + i]
        )
        c.start()
        ld_out.append(c)
    ld_up = pltpu.make_async_copy(upw_hbm, upw, ld_sem.at[14])
    ld_up.start()
    ld_down = pltpu.make_async_copy(downw_hbm, downw, ld_sem.at[15])
    ld_down.start()

    ld_mod.wait()
    modbuf[h] = dot_nt(act_ref[...], modw[...])
    pl.semaphore_wait(barrier, len(partners))
    mod_cps = []
    for dx, dy in DELTAS:
        k = dx * HEADS_Y + dy
        c = rcopy(modbuf.at[h], modbuf.at[h], mod_s.at[k], mod_r.at[k], head_dev(dx, dy))
        c.start()
        mod_cps.append(c)

    ld_tok.wait()
    step = 32
    for i in range(rows // step):
        at = slice(i * step, (i + 1) * step)
        normed[at, :] = layer_norm(tok[at, :].astype(F32))

    for c in mod_cps:
        c.wait_recv()
    local_w = modw.shape[0] // 6
    for s in range(6):
        for p in range(n_head):
            mods[s, :, p * local_w : (p + 1) * local_w] = modbuf[p, :, s * local_w : (s + 1) * local_w]

    views = rows // HD
    for j in range(views):
        shift = mods[0, j : j + 1, :]
        scale = 1.0 + mods[1, j : j + 1, :]
        at = slice(j * HD, (j + 1) * HD)
        h1[at, :] = (normed[at, :] * scale + shift).astype(BF16)

    for c in ld_qkv:
        c.wait()
    lane = lax.broadcasted_iota(jnp.int32, (rows, 2 * HD), 1)
    low = lane < HD
    base = (RADIUS // views) * views
    for i in range(3):
        at = slice(2 * i * HD, 2 * (i + 1) * HD)
        kv = dot_nt(h1[...], wkv[at, :])
        gk = gain_ref[1:2, at]
        ms = jnp.sum(jnp.where(low, kv * kv, 0.0), axis=-1, keepdims=True) * (1.0 / HD)
        kv = kv * jnp.where(low, lax.rsqrt(ms + EPSILON) * gk, 1.0)
        kvb = kv.astype(BF16)
        for j in range(views):
            kv_own[j, :, at] = kvb[j * HD : (j + 1) * HD, :]
            cand[base + j, :, at] = kvb[j * HD : (j + 1) * HD, :]

    kv_cps = []
    for i, d in enumerate((2, -2, 1, -1)):
        c = rcopy(kv_own, cand.at[pl.ds(base - d * views, views)], kv_s.at[i], kv_r.at[i], view_dev(d))
        kv_cps.append(c)

    anchor = anc_ref[0]
    piece = kv_own[lax.rem(anchor, views)]
    owners = jnp.zeros(piece.shape, jnp.int32) + lax.div(anchor, views)
    anc_src[...] = jnp.where(owners == v, piece.astype(F32), 0.0).astype(BF16)
    part_rows = HD // QUAD

    def quarter(ref, index):
        return ref.at[pl.ds(pl.multiple_of(index * part_rows, part_rows), part_rows), :]

    a_cps = []
    for dq in (2, 3, 1):
        peer = (q + dq) % QUAD
        c = rcopy(quarter(anc_src, peer), anc_a.at[dq], aa_s.at[dq], aa_r.at[dq], quad_dev(dq))
        c.start()
        a_cps.append(c)
    for c in kv_cps:
        c.start()

    for i in range(3):
        at = slice(2 * i * HD, 2 * (i + 1) * HD)
        qq = dot_nt(h1[...], wq[at, :])
        gq = gain_ref[0:1, at]
        ms = jnp.sum(qq * qq, axis=-1, keepdims=True) * (1.0 / HD)
        qs[:, at] = (qq * (lax.rsqrt(ms + EPSILON) * gq)).astype(BF16)

    for c in a_cps:
        c.wait_recv()
    mine_q = anc_src[pl.ds(pl.multiple_of(q * part_rows, part_rows), part_rows), :]
    anc_bsrc[...] = mine_q + anc_a[1] + anc_a[2] + anc_a[3]
    b_cps = []
    for dz in sorted(range(1, n_z), key=lambda d: -min(d, n_z - d)):
        c = rcopy(anc_bsrc, anc_b.at[dz], ab_s.at[dz], ab_r.at[dz], z_dev(dz))
        c.start()
        b_cps.append(c)
    for c in b_cps:
        c.wait_recv()
    total = anc_bsrc[...]
    for dz in range(1, n_z):
        total = total + anc_b[dz]
    anc_csrc[...] = total
    anc_full[pl.ds(pl.multiple_of(q * part_rows, part_rows), part_rows), :] = total
    c_cps = []
    for dq in (2, 3, 1):
        c = rcopy(anc_csrc, quarter(anc_full, q), ac_s.at[dq], ac_r.at[dq], quad_dev(dq))
        c.start()
        c_cps.append(c)
    for c in kv_cps:
        c.wait_recv()
    for c in c_cps:
        c.wait_recv()

    full_views = n_view * views
    half = full_views // 2
    slots = adj_ref.shape[1]
    keys = (slots + 2) * HD
    cols = cand.shape[2]
    wlane = lax.broadcasted_iota(jnp.int32, (HD, cols), 1)
    klane = lax.broadcasted_iota(jnp.int32, (1, keys), 1)
    for j in range(views):
        kvg[j, 0:HD, :] = kv_own[j]
        gid = v * views + j
        for s in range(slots):
            off = lax.rem(adj_ref[j, s] - gid + half + full_views, full_views) - half
            at = jnp.minimum(jnp.maximum(base + j + off, 0), cand.shape[0] - 1)
            kvg[j, (s + 1) * HD : (s + 2) * HD, :] = cand[at]
        kvg[j, (slots + 1) * HD : (slots + 2) * HD, :] = anc_full[...]
        qv = qs[j * HD : (j + 1) * HD, :]
        none = jnp.zeros_like(qv)
        qb = jnp.concatenate(
            [
                jnp.where((wlane >= 2 * i * HD) & (wlane < 2 * (i + 1) * HD), qv, none)
                for i in range(3)
            ],
            axis=0,
        )
        sc = dot_nt(qb, kvg[j])
        used = (klane < (cnt_ref[j] + 1) * HD) | (klane >= (slots + 1) * HD)
        sc = jnp.where(used, sc, -1e30)
        top = jnp.max(sc, axis=-1, keepdims=True)
        pw = jnp.exp(sc - top)
        den = jnp.sum(pw, axis=-1, keepdims=True)
        ov = dot_nn(pw.astype(BF16), kvg[j]) * (1.0 / den)
        res = jnp.zeros((HD, cols), F32)
        for i in range(3):
            keep = (wlane >= (2 * i + 1) * HD) & (wlane < 2 * (i + 1) * HD)
            res = jnp.where(keep, ov[i * HD : (i + 1) * HD, :], res)
        att[j * HD : (j + 1) * HD, :] = res.astype(BF16)

    for c in ld_out:
        c.wait()
    tile = 256
    for n in range(width // tile):
        at = slice(n * tile, (n + 1) * tile)
        part[:, at] = dot_nn(att[...], outw[:, at]).astype(BF16)

    def block(ref, index):
        return ref.at[pl.ds(pl.multiple_of(index * blk, blk), blk), :]

    r1_cps = []
    for dx, dy in DELTAS:
        k = dx * HEADS_Y + dy
        c = rcopy(block(part, head_peer(dx, dy)), rs1.at[k], rs1_s.at[k], rs1_r.at[k], head_dev(dx, dy))
        c.start()
        r1_cps.append(c)
    my_rows = pl.ds(pl.multiple_of(h * blk, blk), blk)
    per_view = HD // blk
    my_view = h // per_view
    total = part[my_rows, :].astype(F32)
    for c, (dx, dy) in reversed(list(zip(r1_cps, DELTAS))):
        c.wait_recv()
        total = total + rs1[dx * HEADS_Y + dy].astype(F32)

    def mod_row(s):
        return mods[s, pl.ds(my_view, 1), :]

    res = tok[my_rows, :].astype(F32) + mod_row(2) * total
    resid[...] = res
    h2[0] = (layer_norm(res) * (1.0 + mod_row(4)) + mod_row(3)).astype(BF16)
    g1_cps = []
    for dx, dy in DELTAS:
        k = dx * HEADS_Y + dy
        c = rcopy(h2.at[0], h2.at[k], ag1_s.at[k], ag1_r.at[k], head_dev(dx, dy))
        c.start()
        g1_cps.append(c)
    ld_up.wait()
    ld_down.wait()
    for c in g1_cps:
        c.wait_recv()

    ff = upw.shape[1]
    allh2 = jnp.concatenate([h2[k] for k in range(n_head)], axis=0)
    for n in range(ff // tile):
        at = slice(n * tile, (n + 1) * tile)
        u = dot_nn(allh2, upw[:, at])
        hidden[:, at] = (
            0.5 * u * (1.0 + jnp.tanh(math.sqrt(2.0 / math.pi) * (u + 0.044715 * (u * u * u))))
        ).astype(BF16)
    for n in range(width // tile):
        at = slice(n * tile, (n + 1) * tile)
        part2[:, at] = dot_nn(hidden[...], downw[:, at]).astype(BF16)

    r2_cps = []
    for dx, dy in DELTAS:
        k = dx * HEADS_Y + dy
        bx, by = (HEADS_X - dx) % HEADS_X, (HEADS_Y - dy) % HEADS_Y
        c = rcopy(
            part2.at[pl.ds(k * blk, blk), :], rs2.at[k], rs2_s.at[k], rs2_r.at[k], head_dev(bx, by)
        )
        c.start()
        r2_cps.append(c)
    total = part2[0:blk, :].astype(F32)
    for c, (dx, dy) in reversed(list(zip(r2_cps, DELTAS))):
        c.wait_recv()
        total = total + rs2[dx * HEADS_Y + dy].astype(F32)
    done = (resid[...] + mod_row(5) * total).astype(BF16)
    fin[...] = done
    out_ref[my_rows, :] = done
    g2_cps = []
    for dx, dy in DELTAS:
        k = dx * HEADS_Y + dy
        c = rcopy(fin, block(out_ref, h), ag2_s.at[k], ag2_r.at[k], head_dev(dx, dy))
        c.start()
        g2_cps.append(c)
    for c in g2_cps:
        c.wait_recv()
    for c in mod_cps + kv_cps + a_cps + b_cps + c_cps + r1_cps + g1_cps + r2_cps + g2_cps:
        c.wait_send()


def body(
    n_view,
    tokens,
    timesteps,
    adjacency,
    neighbour_count,
    anchor,
    mod_weight,
    qkv_weight,
    qk_gain,
    out_weight,
    up_weight,
    down_weight,
):
    view_count = timesteps.shape[0]
    rows, width = tokens.shape
    freq = mod_weight.shape[0]
    local_w = qkv_weight.shape[2]
    ff = up_weight.shape[1]
    heads = local_w // HD
    cols = 2 * local_w
    act = jax.nn.silu(time_features(timesteps, freq)).astype(BF16)
    act = jnp.pad(act, ((0, 8 - view_count), (0, 0)))
    gains = qk_gain.reshape(2, heads, HD) * jnp.array([1.0 / math.sqrt(HD), 1.0], F32)[:, None, None]
    gains = jnp.pad(gains, ((0, 0), (0, 0), (0, HD))).reshape(2, cols)
    modw = jnp.transpose(mod_weight, (1, 2, 0)).reshape(6 * local_w, freq)
    qkvw = jnp.transpose(qkv_weight, (1, 2, 0))
    n_head = HEADS_X * HEADS_Y
    blk = rows // n_head
    n_z = n_view // QUAD
    reach = RADIUS // view_count
    cand_rows = (2 * reach + 1) * rows
    slots = adjacency.shape[1]
    quarter = HD // QUAD
    vmem = pltpu.VMEM
    dma = pltpu.SemaphoreType.DMA
    scratch = [
        vmem((rows, width), BF16),
        vmem((6 * local_w, freq), BF16),
        vmem((cols, width), BF16),
        vmem((cols, width), BF16),
        vmem((cols, width), BF16),
        vmem((width, ff), BF16),
        vmem((ff, width), BF16),
        vmem((rows, width), F32),
        vmem((rows, width), BF16),
        vmem((n_head, 8, 6 * local_w), F32),
        vmem((6, 8, width), F32),
        vmem((rows, cols), BF16),
        vmem((view_count, HD, cols), BF16),
        vmem((cand_rows // HD, HD, cols), BF16),
        vmem((view_count, (slots + 2) * HD, cols), BF16),
        vmem((HD, cols), BF16),
        vmem((QUAD, quarter, cols), BF16),
        vmem((n_z, quarter, cols), BF16),
        vmem((quarter, cols), BF16),
        vmem((quarter, cols), BF16),
        vmem((HD, cols), BF16),
        vmem((rows, cols), BF16),
        vmem((rows, width), BF16),
        vmem((n_head, blk, width), BF16),
        vmem((blk, width), F32),
        vmem((n_head, blk, width), BF16),
        vmem((rows, ff), BF16),
        vmem((rows, width), BF16),
        vmem((n_head, blk, width), BF16),
        vmem((blk, width), BF16),
        dma((16,)),
        dma((n_head,)),
        dma((n_head,)),
        dma((4,)),
        dma((4,)),
        dma((QUAD,)),
        dma((QUAD,)),
        dma((n_z,)),
        dma((n_z,)),
        dma((QUAD,)),
        dma((QUAD,)),
    ] + [dma((n_head,))] * 8
    return pl.pallas_call(
        functools.partial(kernel, n_view),
        out_shape=jax.ShapeDtypeStruct((rows, width), BF16),
        in_specs=[
            pl.BlockSpec(memory_space=pltpu.VMEM),
            pl.BlockSpec(memory_space=pltpu.VMEM),
            pl.BlockSpec(memory_space=pltpu.SMEM),
            pl.BlockSpec(memory_space=pltpu.SMEM),
            pl.BlockSpec(memory_space=pltpu.SMEM),
        ]
        + [pl.BlockSpec(memory_space=pl.ANY)] * 6,
        out_specs=pl.BlockSpec(memory_space=pltpu.VMEM),
        scratch_shapes=scratch,
        compiler_params=pltpu.CompilerParams(
            collective_id=0, has_side_effects=True, vmem_limit_bytes=52 * 1024 * 1024
        ),
        name="layer",
    )(
        act,
        gains,
        adjacency,
        neighbour_count,
        anchor,
        tokens,
        modw,
        qkvw,
        out_weight,
        up_weight,
        down_weight,
    )


def solution(mesh):
    return jax.shard_map(
        functools.partial(body, mesh.shape["view"]),
        mesh=mesh,
        in_specs=(
            P("view", None),
            P("view"),
            P("view", None),
            P("view"),
            P(),
            P(None, None, "head"),
            P(None, None, "head"),
            P(None, "head"),
            P("head", None),
            P(None, "head"),
            P("head", None),
        ),
        out_specs=P("view", None),
        check_vma=False,
    )
```

```python
import functools
import math

import jax
import jax.numpy as jnp
from jax import lax
from jax.experimental import pallas as pl
from jax.experimental.pallas import tpu as pltpu
from jax.sharding import PartitionSpec as P

HD = 64
RADIUS = 8
EPSILON = 1e-06
MESH = pl.DeviceIdType.MESH
F32 = jnp.float32
BF16 = jnp.bfloat16

HEADS_X = 4
HEADS_Y = 2
QUAD = 4

DELTAS = [(2, 1), (1, 1), (3, 1), (2, 0), (0, 1), (1, 0), (3, 0)]


def cos_sin(angle):
    turns = jnp.floor(angle * (2.0 / math.pi) + 0.5)
    r = angle - turns * 1.5703125
    r = r - turns * 4.837512969970703125e-4
    r = r - turns * 7.54978995489188216e-8
    s = r * r
    sin = r + r * s * (-1.6666654611e-1 + s * (8.3321608736e-3 - s * 1.9515295891e-4))
    cos = 1.0 - 0.5 * s + s * s * (4.166664568298827e-2 + s * (-1.388731625493765e-3 + s * 2.443315711809948e-5))
    part = turns - 4.0 * jnp.floor(turns * 0.25)
    odd = (part == 1.0) | (part == 3.0)
    base_c = jnp.where(odd, sin, cos)
    base_s = jnp.where(odd, cos, sin)
    return (
        jnp.where((part == 1.0) | (part == 2.0), -base_c, base_c),
        jnp.where((part == 2.0) | (part == 3.0), -base_s, base_s),
    )


def dot_nt(a, b):
    return lax.dot_general(a, b, (((1,), (1,)), ((), ())), preferred_element_type=F32)


def dot_nn(a, b):
    return lax.dot_general(a, b, (((1,), (0,)), ((), ())), preferred_element_type=F32)


def layer_norm(values):
    centre = values - jnp.mean(values, axis=-1, keepdims=True)
    return centre * lax.rsqrt(jnp.mean(centre * centre, axis=-1, keepdims=True) + EPSILON)


def kernel(
    n_view,
    ts_hbm,
    gain_hbm,
    adj_hbm,
    cnt_hbm,
    anc_hbm,
    tok_hbm,
    modw_hbm,
    qkvw_hbm,
    outw_hbm,
    upw_hbm,
    downw_hbm,
    out_ref,
    ts_ref,
    gain_ref,
    adj_ref,
    cnt_ref,
    anc_ref,
    tok,
    modw,
    wq,
    wkv,
    outw,
    upw,
    downw,
    normed,
    h1,
    modbuf,
    mods,
    qs,
    kv_own,
    cand,
    kvg,
    anc_src,
    anc_a,
    anc_b,
    anc_bsrc,
    anc_csrc,
    anc_full,
    att,
    part,
    rs1,
    resid,
    h2,
    hidden,
    part2,
    rs2,
    fin,
    ld_sem,
    mod_s,
    mod_r,
    kv_s,
    kv_r,
    aa_s,
    aa_r,
    ab_s,
    ab_r,
    ac_s,
    ac_r,
    rs1_s,
    rs1_r,
    ag1_s,
    ag1_r,
    rs2_s,
    rs2_r,
    ag2_s,
    ag2_r,
):
    v = lax.axis_index("view")
    h = lax.axis_index("head")
    xx, yh = h // HEADS_Y, h % HEADS_Y
    z, q = v // QUAD, v % QUAD
    n_z = n_view // QUAD
    n_head = HEADS_X * HEADS_Y
    width = tok.shape[1]
    rows = tok.shape[0]
    blk = rows // n_head

    def head_peer(dx, dy):
        return ((xx + dx) % HEADS_X) * HEADS_Y + (yh + dy) % HEADS_Y

    def head_dev(dx, dy):
        return (v, head_peer(dx, dy))

    def view_dev(d):
        return ((v + d + n_view) % n_view, h)

    def quad_dev(dq):
        return (z * QUAD + (q + dq) % QUAD, h)

    def z_dev(dz):
        return (((z + dz) % n_z) * QUAD + q, h)

    def rcopy(src, dst, ss, rs, dev):
        return pltpu.make_async_remote_copy(
            src_ref=src, dst_ref=dst, send_sem=ss, recv_sem=rs, device_id=dev, device_id_type=MESH
        )

    barrier = pltpu.get_barrier_semaphore()
    partners = [head_dev(dx, dy) for dx, dy in DELTAS]
    partners += [view_dev(d) for d in (1, -1, 2, -2)]
    partners += [quad_dev(dq) for dq in range(1, QUAD)]
    partners += [z_dev(dz) for dz in range(1, n_z)]
    for dev in partners:
        pl.semaphore_signal(barrier, inc=1, device_id=dev, device_id_type=MESH)

    ld_ts = pltpu.make_async_copy(ts_hbm, ts_ref, ld_sem.at[16])
    ld_ts.start()
    ld_mod = pltpu.make_async_copy(modw_hbm, modw, ld_sem.at[0])
    ld_mod.start()
    ld_tok = pltpu.make_async_copy(tok_hbm, tok, ld_sem.at[1])
    ld_tok.start()
    ld_small = []
    for i, (src, dst) in enumerate(((gain_hbm, gain_ref), (adj_hbm, adj_ref), (cnt_hbm, cnt_ref), (anc_hbm, anc_ref))):
        c = pltpu.make_async_copy(src, dst, ld_sem.at[17 + i])
        c.start()
        ld_small.append(c)
    zero = jnp.zeros((HD, width), BF16)
    ld_qkv = []
    for i in range(3):
        wq[2 * i * HD + HD : 2 * i * HD + 2 * HD, :] = zero
        outw[2 * i * HD : 2 * i * HD + HD, :] = zero
        for s, (dst, at) in enumerate(
            ((wq, 2 * i * HD), (wkv, 2 * i * HD), (wkv, 2 * i * HD + HD))
        ):
            c = pltpu.make_async_copy(
                qkvw_hbm.at[s, pl.ds(i * HD, HD), :], dst.at[pl.ds(at, HD), :], ld_sem.at[2 + 3 * i + s]
            )
            c.start()
            ld_qkv.append(c)
    ld_out = []
    for i in range(3):
        c = pltpu.make_async_copy(
            outw_hbm.at[pl.ds(i * HD, HD), :], outw.at[pl.ds(2 * i * HD + HD, HD), :], ld_sem.at[11 + i]
        )
        c.start()
        ld_out.append(c)
    ld_up = pltpu.make_async_copy(upw_hbm, upw, ld_sem.at[14])
    ld_up.start()
    ld_down = pltpu.make_async_copy(downw_hbm, downw, ld_sem.at[15])
    ld_down.start()

    views = rows // HD
    ld_ts.wait()
    half_freq = modw.shape[1] // 2
    row8 = lax.broadcasted_iota(jnp.int32, (8, half_freq), 0)
    times = jnp.zeros((8, half_freq), jnp.int32)
    for j in range(views):
        times = jnp.where((row8 == j) | (row8 == j + 4), ts_ref[j], times)
    steps = lax.broadcasted_iota(jnp.int32, (8, half_freq), 1).astype(F32)
    cos, sin = cos_sin(times.astype(F32) * jnp.exp(steps * (-math.log(10000.0) / half_freq)))
    feats = jnp.concatenate([cos, sin], axis=1)
    act = (feats / (1.0 + jnp.exp(-feats))).astype(BF16)
    ld_mod.wait()
    local_w = modw.shape[0] // 6
    first = dot_nt(act, modw[0 : 3 * local_w, :])
    second = dot_nt(act, modw[3 * local_w : 6 * local_w, :])
    row8w = lax.broadcasted_iota(jnp.int32, first.shape, 0)
    modbuf[h] = jnp.where(row8w < 4, first, second).astype(BF16)
    pl.semaphore_wait(barrier, len(partners))
    mod_cps = []
    for dx, dy in DELTAS:
        k = dx * HEADS_Y + dy
        c = rcopy(modbuf.at[h], modbuf.at[h], mod_s.at[k], mod_r.at[k], head_dev(dx, dy))
        c.start()
        mod_cps.append(c)

    ld_tok.wait()
    step = 32
    for i in range(rows // step):
        at = slice(i * step, (i + 1) * step)
        normed[at, :] = layer_norm(tok[at, :].astype(F32))

    for c in mod_cps:
        c.wait_recv()
    for p in range(n_head):
        got = modbuf[p].astype(F32)
        for s in range(3):
            mods[s, :, p * local_w : (p + 1) * local_w] = got[:, s * local_w : (s + 1) * local_w]

    for j in range(views):
        shift = mods[0, j : j + 1, :]
        scale = 1.0 + mods[1, j : j + 1, :]
        at = slice(j * HD, (j + 1) * HD)
        h1[at, :] = (normed[at, :] * scale + shift).astype(BF16)

    for c in ld_qkv + ld_small:
        c.wait()
    lane = lax.broadcasted_iota(jnp.int32, (rows, 2 * HD), 1)
    low = lane < HD
    base = (RADIUS // views) * views
    for i in range(3):
        at = slice(2 * i * HD, 2 * (i + 1) * HD)
        kv = dot_nt(h1[...], wkv[at, :])
        gk = jnp.concatenate([gain_ref[1:2, i * HD : (i + 1) * HD], jnp.ones((1, HD), F32)], axis=1)
        ms = jnp.sum(jnp.where(low, kv * kv, 0.0), axis=-1, keepdims=True) * (1.0 / HD)
        kv = kv * jnp.where(low, lax.rsqrt(ms + EPSILON) * gk, 1.0)
        kvb = kv.astype(BF16)
        for j in range(views):
            kv_own[j, :, at] = kvb[j * HD : (j + 1) * HD, :]
            cand[base + j, :, at] = kvb[j * HD : (j + 1) * HD, :]

    core = v % 2
    mate = view_dev(1 - 2 * core)
    kv_cps = []
    fwd_cps = []

    def send_kv(j):
        for i, (dst, dev) in enumerate(
            (
                (base - 2 * views + j, view_dev(2)),
                (base + 2 * views + j, view_dev(-2)),
                (base - views + 2 * views * core + j, mate),
            )
        ):
            c = rcopy(kv_own.at[j], cand.at[dst], kv_s.at[i, j], kv_r.at[i, j], dev)
            c.start()
            kv_cps.append(c)

    def forward_kv(j):
        got = base + 2 * views - 4 * views * core + j
        rcopy(kv_own.at[j], cand.at[got], kv_s.at[0, j], kv_r.at[1 - core, j], mate).wait_recv()
        c = rcopy(
            cand.at[got], cand.at[base + views - 2 * views * core + j], kv_s.at[3, j], kv_r.at[3, j], mate
        )
        c.start()
        fwd_cps.append(c)

    anchor = anc_ref[0]
    piece = kv_own[lax.rem(anchor, views)]
    owners = jnp.zeros(piece.shape, jnp.int32) + lax.div(anchor, views)
    anc_src[...] = jnp.where(owners == v, piece.astype(F32), 0.0).astype(BF16)
    part_rows = HD // QUAD

    def quarter(ref, index):
        return ref.at[pl.ds(pl.multiple_of(index * part_rows, part_rows), part_rows), :]

    a_cps = []
    for dq in (2, 3, 1):
        peer = (q + dq) % QUAD
        c = rcopy(quarter(anc_src, peer), anc_a.at[dq], aa_s.at[dq], aa_r.at[dq], quad_dev(dq))
        c.start()
        a_cps.append(c)
    send_kv(0)
    send_kv(1)

    for i in range(3):
        at = slice(2 * i * HD, 2 * (i + 1) * HD)
        qq = dot_nt(h1[...], wq[at, :])
        gq = gain_ref[0:1, i * HD : (i + 1) * HD] * (1.0 / math.sqrt(HD))
        gq = jnp.concatenate([gq, jnp.zeros((1, HD), F32)], axis=1)
        ms = jnp.sum(qq * qq, axis=-1, keepdims=True) * (1.0 / HD)
        qs[:, at] = (qq * (lax.rsqrt(ms + EPSILON) * gq)).astype(BF16)

    for c in a_cps:
        c.wait_recv()
    mine_q = anc_src[pl.ds(pl.multiple_of(q * part_rows, part_rows), part_rows), :]
    anc_bsrc[...] = mine_q + anc_a[1] + anc_a[2] + anc_a[3]
    b_cps = []
    for dz in sorted(range(1, n_z), key=lambda d: -min(d, n_z - d)):
        c = rcopy(anc_bsrc, anc_b.at[dz], ab_s.at[dz], ab_r.at[dz], z_dev(dz))
        c.start()
        b_cps.append(c)
    for j in range(2, views):
        send_kv(j)
    forward_kv(0)
    forward_kv(1)
    for c in b_cps:
        c.wait_recv()
    total = anc_bsrc[...]
    for dz in range(1, n_z):
        total = total + anc_b[dz]
    anc_csrc[...] = total
    anc_full[pl.ds(pl.multiple_of(q * part_rows, part_rows), part_rows), :] = total
    c_cps = []
    for dq in (2, 3, 1):
        c = rcopy(anc_csrc, quarter(anc_full, q), ac_s.at[dq], ac_r.at[dq], quad_dev(dq))
        c.start()
        c_cps.append(c)
    for j in range(2, views):
        forward_kv(j)
    for j in range(views):
        got = base - 2 * views + 4 * views * core + j
        rcopy(kv_own.at[j], cand.at[got], kv_s.at[0, j], kv_r.at[core, j], mate).wait_recv()
        kv_cps[3 * j + 2].wait_recv()
        fwd_cps[j].wait_recv()
    for c in c_cps:
        c.wait_recv()

    full_views = n_view * views
    half = full_views // 2
    slots = adj_ref.shape[1]
    keys = (slots + 2) * HD
    cols = cand.shape[2]
    wlane = lax.broadcasted_iota(jnp.int32, (HD, cols), 1)
    klane = lax.broadcasted_iota(jnp.int32, (1, keys), 1)
    for j in range(views):
        kvg[j, 0:HD, :] = kv_own[j]
        gid = v * views + j
        for s in range(slots):
            off = lax.rem(adj_ref[j, s] - gid + half + full_views, full_views) - half
            at = jnp.minimum(jnp.maximum(base + j + off, 0), cand.shape[0] - 1)
            kvg[j, (s + 1) * HD : (s + 2) * HD, :] = cand[at]
        kvg[j, (slots + 1) * HD : (slots + 2) * HD, :] = anc_full[...]
        qv = qs[j * HD : (j + 1) * HD, :]
        none = jnp.zeros_like(qv)
        qb = jnp.concatenate(
            [
                jnp.where((wlane >= 2 * i * HD) & (wlane < 2 * (i + 1) * HD), qv, none)
                for i in range(3)
            ],
            axis=0,
        )
        sc = dot_nt(qb, kvg[j])
        used = (klane < (cnt_ref[j] + 1) * HD) | (klane >= (slots + 1) * HD)
        sc = jnp.where(used, sc, -1e30)
        top = jnp.max(sc, axis=-1, keepdims=True)
        pw = jnp.exp(sc - top)
        den = jnp.sum(pw, axis=-1, keepdims=True)
        ov = dot_nn(pw.astype(BF16), kvg[j]) * (1.0 / den)
        res = jnp.zeros((HD, cols), F32)
        for i in range(3):
            keep = (wlane >= (2 * i + 1) * HD) & (wlane < 2 * (i + 1) * HD)
            res = jnp.where(keep, ov[i * HD : (i + 1) * HD, :], res)
        att[j * HD : (j + 1) * HD, :] = res.astype(BF16)

    for c in ld_out:
        c.wait()
    tile = 256
    for n in range(width // tile):
        at = slice(n * tile, (n + 1) * tile)
        part[:, at] = dot_nn(att[...], outw[:, at]).astype(BF16)

    def block(ref, index):
        return ref.at[pl.ds(pl.multiple_of(index * blk, blk), blk), :]

    r1_cps = []
    for dx, dy in DELTAS:
        k = dx * HEADS_Y + dy
        c = rcopy(block(part, head_peer(dx, dy)), rs1.at[k], rs1_s.at[k], rs1_r.at[k], head_dev(dx, dy))
        c.start()
        r1_cps.append(c)
    my_rows = pl.ds(pl.multiple_of(h * blk, blk), blk)
    per_view = HD // blk
    my_view = h // per_view
    total = part[my_rows, :].astype(F32)
    for c, (dx, dy) in reversed(list(zip(r1_cps, DELTAS))):
        c.wait_recv()
        total = total + rs1[dx * HEADS_Y + dy].astype(F32)

    def mod_row(s):
        return mods[s % 3, pl.ds(my_view + 4 * (s // 3), 1), :]

    res = tok[my_rows, :].astype(F32) + mod_row(2) * total
    resid[...] = res
    h2[0] = (layer_norm(res) * (1.0 + mod_row(4)) + mod_row(3)).astype(BF16)
    g1_cps = []
    for dx, dy in DELTAS:
        k = dx * HEADS_Y + dy
        c = rcopy(h2.at[0], h2.at[k], ag1_s.at[k], ag1_r.at[k], head_dev(dx, dy))
        c.start()
        g1_cps.append(c)
    ld_up.wait()
    ld_down.wait()
    for c in g1_cps:
        c.wait_recv()

    ff = upw.shape[1]
    allh2 = jnp.concatenate([h2[k] for k in range(n_head)], axis=0)
    for n in range(ff // tile):
        at = slice(n * tile, (n + 1) * tile)
        u = dot_nn(allh2, upw[:, at])
        hidden[:, at] = (
            0.5 * u * (1.0 + jnp.tanh(math.sqrt(2.0 / math.pi) * (u + 0.044715 * (u * u * u))))
        ).astype(BF16)
    for n in range(width // tile):
        at = slice(n * tile, (n + 1) * tile)
        part2[:, at] = dot_nn(hidden[...], downw[:, at]).astype(BF16)

    r2_cps = []
    for dx, dy in DELTAS:
        k = dx * HEADS_Y + dy
        bx, by = (HEADS_X - dx) % HEADS_X, (HEADS_Y - dy) % HEADS_Y
        c = rcopy(
            part2.at[pl.ds(k * blk, blk), :], rs2.at[k], rs2_s.at[k], rs2_r.at[k], head_dev(bx, by)
        )
        c.start()
        r2_cps.append(c)
    total = part2[0:blk, :].astype(F32)
    for c, (dx, dy) in reversed(list(zip(r2_cps, DELTAS))):
        c.wait_recv()
        total = total + rs2[dx * HEADS_Y + dy].astype(F32)
    done = (resid[...] + mod_row(5) * total).astype(BF16)
    fin[...] = done
    out_ref[my_rows, :] = done
    g2_cps = []
    for dx, dy in DELTAS:
        k = dx * HEADS_Y + dy
        c = rcopy(fin, block(out_ref, h), ag2_s.at[k], ag2_r.at[k], head_dev(dx, dy))
        c.start()
        g2_cps.append(c)
    for c in g2_cps:
        c.wait_recv()
    for c in mod_cps + kv_cps + fwd_cps + a_cps + b_cps + c_cps + r1_cps + g1_cps + r2_cps + g2_cps:
        c.wait_send()


def body(
    n_view,
    tokens,
    timesteps,
    adjacency,
    neighbour_count,
    anchor,
    mod_weight,
    qkv_weight,
    qk_gain,
    out_weight,
    up_weight,
    down_weight,
):
    view_count = timesteps.shape[0]
    rows, width = tokens.shape
    freq = mod_weight.shape[0]
    local_w = qkv_weight.shape[2]
    ff = up_weight.shape[1]
    cols = 2 * local_w
    modw = jnp.transpose(mod_weight, (1, 2, 0)).reshape(6 * local_w, freq)
    qkvw = jnp.transpose(qkv_weight, (1, 2, 0))
    n_head = HEADS_X * HEADS_Y
    blk = rows // n_head
    n_z = n_view // QUAD
    reach = RADIUS // view_count
    cand_rows = (2 * reach + 1) * rows
    slots = adjacency.shape[1]
    quarter = HD // QUAD
    vmem = pltpu.VMEM
    dma = pltpu.SemaphoreType.DMA
    scratch = [
        pltpu.SMEM(timesteps.shape, jnp.int32),
        vmem(qk_gain.shape, F32),
        pltpu.SMEM(adjacency.shape, jnp.int32),
        pltpu.SMEM(neighbour_count.shape, jnp.int32),
        pltpu.SMEM(anchor.shape, jnp.int32),
        vmem((rows, width), BF16),
        vmem((6 * local_w, freq), BF16),
        vmem((cols, width), BF16),
        vmem((cols, width), BF16),
        vmem((cols, width), BF16),
        vmem((width, ff), BF16),
        vmem((ff, width), BF16),
        vmem((rows, width), F32),
        vmem((rows, width), BF16),
        vmem((n_head, 8, 3 * local_w), BF16),
        vmem((3, 8, width), F32),
        vmem((rows, cols), BF16),
        vmem((view_count, HD, cols), BF16),
        vmem((cand_rows // HD, HD, cols), BF16),
        vmem((view_count, (slots + 2) * HD, cols), BF16),
        vmem((HD, cols), BF16),
        vmem((QUAD, quarter, cols), BF16),
        vmem((n_z, quarter, cols), BF16),
        vmem((quarter, cols), BF16),
        vmem((quarter, cols), BF16),
        vmem((HD, cols), BF16),
        vmem((rows, cols), BF16),
        vmem((rows, width), BF16),
        vmem((n_head, blk, width), BF16),
        vmem((blk, width), F32),
        vmem((n_head, blk, width), BF16),
        vmem((rows, ff), BF16),
        vmem((rows, width), BF16),
        vmem((n_head, blk, width), BF16),
        vmem((blk, width), BF16),
        dma((21,)),
        dma((n_head,)),
        dma((n_head,)),
        dma((4, view_count)),
        dma((4, view_count)),
        dma((QUAD,)),
        dma((QUAD,)),
        dma((n_z,)),
        dma((n_z,)),
        dma((QUAD,)),
        dma((QUAD,)),
    ] + [dma((n_head,))] * 8
    return pl.pallas_call(
        functools.partial(kernel, n_view),
        out_shape=jax.ShapeDtypeStruct((rows, width), BF16),
        in_specs=[pl.BlockSpec(memory_space=pl.ANY)] * 11,
        out_specs=pl.BlockSpec(memory_space=pltpu.VMEM),
        scratch_shapes=scratch,
        compiler_params=pltpu.CompilerParams(
            collective_id=0, has_side_effects=True, vmem_limit_bytes=67043328
        ),
        name="layer",
    )(
        timesteps,
        qk_gain,
        adjacency,
        neighbour_count,
        anchor,
        tokens,
        modw,
        qkvw,
        out_weight,
        up_weight,
        down_weight,
    )


def solution(mesh):
    return jax.shard_map(
        functools.partial(body, mesh.shape["view"]),
        mesh=mesh,
        in_specs=(
            P("view", None),
            P("view"),
            P("view", None),
            P("view"),
            P(),
            P(None, None, "head"),
            P(None, None, "head"),
            P(None, "head"),
            P("head", None),
            P(None, "head"),
            P("head", None),
        ),
        out_specs=P("view", None),
        check_vma=False,
    )
```

```python
import functools
import math

import jax
import jax.numpy as jnp
from jax import lax
from jax.experimental import pallas as pl
from jax.experimental.pallas import tpu as pltpu
from jax.sharding import PartitionSpec as P

HD = 64
RADIUS = 8
EPSILON = 1e-06
MESH = pl.DeviceIdType.MESH
F32 = jnp.float32
BF16 = jnp.bfloat16

HEADS_X = 4
HEADS_Y = 2
QUAD = 4
CHUNKS = 2

DELTAS = [(2, 1), (1, 1), (3, 1), (2, 0), (0, 1), (1, 0), (3, 0)]


def cos_sin(angle):
    turns = jnp.floor(angle * (2.0 / math.pi) + 0.5)
    r = angle - turns * 1.5703125
    r = r - turns * 4.837512969970703125e-4
    r = r - turns * 7.54978995489188216e-8
    s = r * r
    sin = r + r * s * (-1.6666654611e-1 + s * (8.3321608736e-3 - s * 1.9515295891e-4))
    cos = 1.0 - 0.5 * s + s * s * (4.166664568298827e-2 + s * (-1.388731625493765e-3 + s * 2.443315711809948e-5))
    part = turns - 4.0 * jnp.floor(turns * 0.25)
    odd = (part == 1.0) | (part == 3.0)
    base_c = jnp.where(odd, sin, cos)
    base_s = jnp.where(odd, cos, sin)
    return (
        jnp.where((part == 1.0) | (part == 2.0), -base_c, base_c),
        jnp.where((part == 2.0) | (part == 3.0), -base_s, base_s),
    )


def dot_nt(a, b):
    return lax.dot_general(a, b, (((1,), (1,)), ((), ())), preferred_element_type=F32)


def dot_nn(a, b):
    return lax.dot_general(a, b, (((1,), (0,)), ((), ())), preferred_element_type=F32)


def layer_norm(values):
    centre = values - jnp.mean(values, axis=-1, keepdims=True)
    return centre * lax.rsqrt(jnp.mean(centre * centre, axis=-1, keepdims=True) + EPSILON)


def kernel(
    n_view,
    ts_hbm,
    gain_hbm,
    adj_hbm,
    cnt_hbm,
    anc_hbm,
    tok_hbm,
    modw_hbm,
    qkvw_hbm,
    outw_hbm,
    upw_hbm,
    downw_hbm,
    out_ref,
    ts_ref,
    gain_ref,
    adj_ref,
    cnt_ref,
    anc_ref,
    tok,
    modw,
    wq,
    wkv,
    outw,
    upw,
    downw,
    normed,
    h1,
    modbuf,
    mods,
    qs,
    kv_own,
    cand,
    kvg,
    anc_src,
    anc_a,
    anc_b,
    anc_bsrc,
    anc_csrc,
    anc_full,
    att,
    part,
    rs1,
    resid,
    h2,
    hidden,
    part2,
    rs2,
    fin,
    ld_sem,
    mod_s,
    mod_r,
    kv_s,
    kv_r,
    aa_s,
    aa_r,
    ab_s,
    ab_r,
    ac_s,
    ac_r,
    rs1_s,
    rs1_r,
    ag1_s,
    ag1_r,
    rs2_s,
    rs2_r,
    ag2_s,
    ag2_r,
):
    v = lax.axis_index("view")
    h = lax.axis_index("head")
    xx, yh = h // HEADS_Y, h % HEADS_Y
    z, q = v // QUAD, v % QUAD
    n_z = n_view // QUAD
    n_head = HEADS_X * HEADS_Y
    width = tok.shape[1]
    rows = tok.shape[0]

    def head_peer(dx, dy):
        return ((xx + dx) % HEADS_X) * HEADS_Y + (yh + dy) % HEADS_Y

    def head_dev(dx, dy):
        return (v, head_peer(dx, dy))

    def view_dev(d):
        return ((v + d + n_view) % n_view, h)

    def quad_dev(dq):
        return (z * QUAD + (q + dq) % QUAD, h)

    def z_dev(dz):
        return (((z + dz) % n_z) * QUAD + q, h)

    def rcopy(src, dst, ss, rs, dev):
        return pltpu.make_async_remote_copy(
            src_ref=src, dst_ref=dst, send_sem=ss, recv_sem=rs, device_id=dev, device_id_type=MESH
        )

    barrier = pltpu.get_barrier_semaphore()
    partners = [head_dev(dx, dy) for dx, dy in DELTAS]
    partners += [view_dev(d) for d in (1, -1, 2, -2)]
    partners += [quad_dev(dq) for dq in range(1, QUAD)]
    partners += [z_dev(dz) for dz in range(1, n_z)]
    for dev in partners:
        pl.semaphore_signal(barrier, inc=1, device_id=dev, device_id_type=MESH)

    ld_ts = pltpu.make_async_copy(ts_hbm, ts_ref, ld_sem.at[16])
    ld_ts.start()
    ld_mod = pltpu.make_async_copy(modw_hbm, modw, ld_sem.at[0])
    ld_mod.start()
    ld_tok = pltpu.make_async_copy(tok_hbm, tok, ld_sem.at[1])
    ld_tok.start()
    ld_small = []
    for i, (src, dst) in enumerate(((gain_hbm, gain_ref), (adj_hbm, adj_ref), (cnt_hbm, cnt_ref), (anc_hbm, anc_ref))):
        c = pltpu.make_async_copy(src, dst, ld_sem.at[17 + i])
        c.start()
        ld_small.append(c)
    zero = jnp.zeros((HD, width), BF16)
    ld_qkv = []
    for i in range(3):
        wq[2 * i * HD + HD : 2 * i * HD + 2 * HD, :] = zero
        outw[2 * i * HD : 2 * i * HD + HD, :] = zero
        for s, (dst, at) in enumerate(
            ((wq, 2 * i * HD), (wkv, 2 * i * HD), (wkv, 2 * i * HD + HD))
        ):
            c = pltpu.make_async_copy(
                qkvw_hbm.at[s, pl.ds(i * HD, HD), :], dst.at[pl.ds(at, HD), :], ld_sem.at[2 + 3 * i + s]
            )
            c.start()
            ld_qkv.append(c)
    ld_out = []
    for i in range(3):
        c = pltpu.make_async_copy(
            outw_hbm.at[pl.ds(i * HD, HD), :], outw.at[pl.ds(2 * i * HD + HD, HD), :], ld_sem.at[11 + i]
        )
        c.start()
        ld_out.append(c)
    ld_up = pltpu.make_async_copy(upw_hbm, upw, ld_sem.at[14])
    ld_up.start()
    ld_down = pltpu.make_async_copy(downw_hbm, downw, ld_sem.at[15])
    ld_down.start()

    views = rows // HD
    ld_ts.wait()
    half_freq = modw.shape[1] // 2
    row8 = lax.broadcasted_iota(jnp.int32, (8, half_freq), 0)
    times = jnp.zeros((8, half_freq), jnp.int32)
    for j in range(views):
        times = jnp.where((row8 == j) | (row8 == j + 4), ts_ref[j], times)
    steps = lax.broadcasted_iota(jnp.int32, (8, half_freq), 1).astype(F32)
    cos, sin = cos_sin(times.astype(F32) * jnp.exp(steps * (-math.log(10000.0) / half_freq)))
    feats = jnp.concatenate([cos, sin], axis=1)
    act = (feats / (1.0 + jnp.exp(-feats))).astype(BF16)
    ld_mod.wait()
    local_w = modw.shape[0] // 6
    first = dot_nt(act, modw[0 : 3 * local_w, :])
    second = dot_nt(act, modw[3 * local_w : 6 * local_w, :])
    row8w = lax.broadcasted_iota(jnp.int32, first.shape, 0)
    modbuf[h] = jnp.where(row8w < 4, first, second).astype(BF16)
    pl.semaphore_wait(barrier, len(partners))
    mod_cps = []
    for dx, dy in DELTAS:
        k = dx * HEADS_Y + dy
        c = rcopy(modbuf.at[h], modbuf.at[h], mod_s.at[k], mod_r.at[k], head_dev(dx, dy))
        c.start()
        mod_cps.append(c)

    ld_tok.wait()
    step = 32
    for i in range(rows // step):
        at = slice(i * step, (i + 1) * step)
        normed[at, :] = layer_norm(tok[at, :].astype(F32))

    for c in mod_cps:
        c.wait_recv()
    for p in range(n_head):
        got = modbuf[p].astype(F32)
        for s in range(3):
            mods[s, :, p * local_w : (p + 1) * local_w] = got[:, s * local_w : (s + 1) * local_w]

    for j in range(views):
        shift = mods[0, j : j + 1, :]
        scale = 1.0 + mods[1, j : j + 1, :]
        at = slice(j * HD, (j + 1) * HD)
        h1[at, :] = (normed[at, :] * scale + shift).astype(BF16)

    for c in ld_qkv + ld_small:
        c.wait()
    lane = lax.broadcasted_iota(jnp.int32, (rows, 2 * HD), 1)
    low = lane < HD
    base = (RADIUS // views) * views
    for i in range(3):
        at = slice(2 * i * HD, 2 * (i + 1) * HD)
        kv = dot_nt(h1[...], wkv[at, :])
        gk = jnp.concatenate([gain_ref[1:2, i * HD : (i + 1) * HD], jnp.ones((1, HD), F32)], axis=1)
        ms = jnp.sum(jnp.where(low, kv * kv, 0.0), axis=-1, keepdims=True) * (1.0 / HD)
        kv = kv * jnp.where(low, lax.rsqrt(ms + EPSILON) * gk, 1.0)
        kvb = kv.astype(BF16)
        for j in range(views):
            kv_own[j, :, at] = kvb[j * HD : (j + 1) * HD, :]
            cand[base + j, :, at] = kvb[j * HD : (j + 1) * HD, :]

    core = v % 2
    mate = view_dev(1 - 2 * core)
    kv_cps = []
    fwd_cps = []

    def send_kv(j):
        for i, (dst, dev) in enumerate(
            (
                (base - 2 * views + j, view_dev(2)),
                (base + 2 * views + j, view_dev(-2)),
                (base - views + 2 * views * core + j, mate),
            )
        ):
            c = rcopy(kv_own.at[j], cand.at[dst], kv_s.at[i, j], kv_r.at[i, j], dev)
            c.start()
            kv_cps.append(c)

    def forward_kv(j):
        got = base + 2 * views - 4 * views * core + j
        rcopy(kv_own.at[j], cand.at[got], kv_s.at[0, j], kv_r.at[1 - core, j], mate).wait_recv()
        c = rcopy(
            cand.at[got], cand.at[base + views - 2 * views * core + j], kv_s.at[3, j], kv_r.at[3, j], mate
        )
        c.start()
        fwd_cps.append(c)

    anchor = anc_ref[0]
    piece = kv_own[lax.rem(anchor, views)]
    owners = jnp.zeros(piece.shape, jnp.int32) + lax.div(anchor, views)
    anc_src[...] = jnp.where(owners == v, piece.astype(F32), 0.0).astype(BF16)
    part_rows = HD // QUAD

    def quarter(ref, index):
        return ref.at[pl.ds(pl.multiple_of(index * part_rows, part_rows), part_rows), :]

    a_cps = []
    for dq in (2, 3, 1):
        peer = (q + dq) % QUAD
        c = rcopy(quarter(anc_src, peer), anc_a.at[dq], aa_s.at[dq], aa_r.at[dq], quad_dev(dq))
        c.start()
        a_cps.append(c)
    send_kv(0)
    send_kv(1)

    for i in range(3):
        at = slice(2 * i * HD, 2 * (i + 1) * HD)
        qq = dot_nt(h1[...], wq[at, :])
        gq = gain_ref[0:1, i * HD : (i + 1) * HD] * (1.0 / math.sqrt(HD))
        gq = jnp.concatenate([gq, jnp.zeros((1, HD), F32)], axis=1)
        ms = jnp.sum(qq * qq, axis=-1, keepdims=True) * (1.0 / HD)
        qs[:, at] = (qq * (lax.rsqrt(ms + EPSILON) * gq)).astype(BF16)

    for c in a_cps:
        c.wait_recv()
    mine_q = anc_src[pl.ds(pl.multiple_of(q * part_rows, part_rows), part_rows), :]
    anc_bsrc[...] = mine_q + anc_a[1] + anc_a[2] + anc_a[3]
    b_cps = []
    for dz in sorted(range(1, n_z), key=lambda d: -min(d, n_z - d)):
        c = rcopy(anc_bsrc, anc_b.at[dz], ab_s.at[dz], ab_r.at[dz], z_dev(dz))
        c.start()
        b_cps.append(c)
    for j in range(2, views):
        send_kv(j)
    forward_kv(0)
    forward_kv(1)
    for c in b_cps:
        c.wait_recv()
    total = anc_bsrc[...]
    for dz in range(1, n_z):
        total = total + anc_b[dz]
    anc_csrc[...] = total
    anc_full[pl.ds(pl.multiple_of(q * part_rows, part_rows), part_rows), :] = total
    c_cps = []
    for dq in (2, 3, 1):
        c = rcopy(anc_csrc, quarter(anc_full, q), ac_s.at[dq], ac_r.at[dq], quad_dev(dq))
        c.start()
        c_cps.append(c)
    for j in range(2, views):
        forward_kv(j)
    for j in range(views):
        got = base - 2 * views + 4 * views * core + j
        rcopy(kv_own.at[j], cand.at[got], kv_s.at[0, j], kv_r.at[core, j], mate).wait_recv()
        kv_cps[3 * j + 2].wait_recv()
        fwd_cps[j].wait_recv()
    for c in c_cps:
        c.wait_recv()

    full_views = n_view * views
    half = full_views // 2
    slots = adj_ref.shape[1]
    keys = (slots + 2) * HD
    cols = cand.shape[2]
    wlane = lax.broadcasted_iota(jnp.int32, (HD, cols), 1)
    klane = lax.broadcasted_iota(jnp.int32, (1, keys), 1)
    def attention(j):
        kvg[j, 0:HD, :] = kv_own[j]
        gid = v * views + j
        for s in range(slots):
            off = lax.rem(adj_ref[j, s] - gid + half + full_views, full_views) - half
            at = jnp.minimum(jnp.maximum(base + j + off, 0), cand.shape[0] - 1)
            kvg[j, (s + 1) * HD : (s + 2) * HD, :] = cand[at]
        kvg[j, (slots + 1) * HD : (slots + 2) * HD, :] = anc_full[...]
        qv = qs[j * HD : (j + 1) * HD, :]
        none = jnp.zeros_like(qv)
        qb = jnp.concatenate(
            [
                jnp.where((wlane >= 2 * i * HD) & (wlane < 2 * (i + 1) * HD), qv, none)
                for i in range(3)
            ],
            axis=0,
        )
        sc = dot_nt(qb, kvg[j])
        used = (klane < (cnt_ref[j] + 1) * HD) | (klane >= (slots + 1) * HD)
        sc = jnp.where(used, sc, -1e30)
        top = jnp.max(sc, axis=-1, keepdims=True)
        pw = jnp.exp(sc - top)
        den = jnp.sum(pw, axis=-1, keepdims=True)
        ov = dot_nn(pw.astype(BF16), kvg[j]) * (1.0 / den)
        res = jnp.zeros((HD, cols), F32)
        for i in range(3):
            keep = (wlane >= (2 * i + 1) * HD) & (wlane < 2 * (i + 1) * HD)
            res = jnp.where(keep, ov[i * HD : (i + 1) * HD, :], res)
        att[j * HD : (j + 1) * HD, :] = res.astype(BF16)

    tile = 256
    crows = rows // CHUNKS
    blk = crows // n_head
    ff = upw.shape[1]

    def rows_at(start, size):
        return pl.ds(pl.multiple_of(start, size), size)

    def mod_row(s, view):
        return mods[s % 3, pl.ds(view + 4 * (s // 3), 1), :]

    r1_cps, g1_cps, r2_cps, g2_cps = ([[] for _ in range(CHUNKS)] for _ in range(4))

    def project(c):
        span = slice(c * crows, (c + 1) * crows)
        for n in range(width // tile):
            at = slice(n * tile, (n + 1) * tile)
            part[span, at] = dot_nn(att[span, :], outw[:, at]).astype(BF16)
        for dx, dy in DELTAS:
            k = dx * HEADS_Y + dy
            src = part.at[rows_at(c * crows + head_peer(dx, dy) * blk, blk), :]
            r1_cps[c].append(rcopy(src, rs1.at[k, c], rs1_s.at[k, c], rs1_r.at[k, c], head_dev(dx, dy)))
            r1_cps[c][-1].start()

    def second_norm(c):
        mine = rows_at(c * crows + h * blk, blk)
        view = (c * crows + h * blk) // HD
        total = part[mine, :].astype(F32)
        for cp in reversed(r1_cps[c]):
            cp.wait_recv()
        for k in range(1, n_head):
            total = total + rs1[k, c].astype(F32)
        res = tok[mine, :].astype(F32) + mod_row(2, view) * total
        resid[c] = res
        h2[c, 0:blk, :] = (layer_norm(res) * (1.0 + mod_row(4, view)) + mod_row(3, view)).astype(BF16)
        for dx, dy in DELTAS:
            k = dx * HEADS_Y + dy
            src, dst = h2.at[c, pl.ds(0, blk), :], h2.at[c, pl.ds(k * blk, blk), :]
            g1_cps[c].append(rcopy(src, dst, ag1_s.at[k, c], ag1_r.at[k, c], head_dev(dx, dy)))
            g1_cps[c][-1].start()

    def feed_forward(c):
        for cp in reversed(g1_cps[c]):
            cp.wait_recv()
        span = slice(c * crows, (c + 1) * crows)
        for n in range(ff // tile):
            at = slice(n * tile, (n + 1) * tile)
            u = dot_nn(h2[c], upw[:, at])
            hidden[span, at] = (
                0.5 * u * (1.0 + jnp.tanh(math.sqrt(2.0 / math.pi) * (u + 0.044715 * (u * u * u))))
            ).astype(BF16)
        for n in range(width // tile):
            at = slice(n * tile, (n + 1) * tile)
            part2[span, at] = dot_nn(hidden[span, :], downw[:, at]).astype(BF16)
        for dx, dy in DELTAS:
            bx, by = (HEADS_X - dx) % HEADS_X, (HEADS_Y - dy) % HEADS_Y
            k = bx * HEADS_Y + by
            src = part2.at[pl.ds(c * crows + k * blk, blk), :]
            r2_cps[c].append(rcopy(src, rs2.at[k, c], rs2_s.at[k, c], rs2_r.at[k, c], head_dev(dx, dy)))
            r2_cps[c][-1].start()

    def finish(c):
        view = (c * crows + h * blk) // HD
        total = part2[c * crows : c * crows + blk, :].astype(F32)
        for cp in reversed(r2_cps[c]):
            cp.wait_recv()
        for k in range(1, n_head):
            total = total + rs2[k, c].astype(F32)
        done = (resid[c] + mod_row(5, view) * total).astype(BF16)
        fin[c] = done
        mine = rows_at(c * crows + h * blk, blk)
        out_ref[mine, :] = done
        for dx, dy in DELTAS:
            k = dx * HEADS_Y + dy
            g2_cps[c].append(rcopy(fin.at[c], out_ref.at[mine, :], ag2_s.at[k, c], ag2_r.at[k, c], head_dev(dx, dy)))
            g2_cps[c][-1].start()

    for c in ld_out:
        c.wait()
    for c in range(CHUNKS):
        for j in range(c * crows // HD, (c + 1) * crows // HD):
            attention(j)
        project(c)
    for c in range(CHUNKS):
        second_norm(c)
    ld_up.wait()
    ld_down.wait()
    for c in range(CHUNKS):
        feed_forward(c)
    for c in range(CHUNKS):
        finish(c)
    for c in range(CHUNKS):
        for cp in g2_cps[c]:
            cp.wait_recv()
    rest = [cp for phase in (r1_cps, g1_cps, r2_cps, g2_cps) for group in phase for cp in group]
    for c in mod_cps + kv_cps + fwd_cps + a_cps + b_cps + c_cps + rest:
        c.wait_send()


def body(
    n_view,
    tokens,
    timesteps,
    adjacency,
    neighbour_count,
    anchor,
    mod_weight,
    qkv_weight,
    qk_gain,
    out_weight,
    up_weight,
    down_weight,
):
    view_count = timesteps.shape[0]
    rows, width = tokens.shape
    freq = mod_weight.shape[0]
    local_w = qkv_weight.shape[2]
    ff = up_weight.shape[1]
    cols = 2 * local_w
    modw = jnp.transpose(mod_weight, (1, 2, 0)).reshape(6 * local_w, freq)
    qkvw = jnp.transpose(qkv_weight, (1, 2, 0))
    n_head = HEADS_X * HEADS_Y
    blk = rows // n_head // CHUNKS
    n_z = n_view // QUAD
    reach = RADIUS // view_count
    cand_rows = (2 * reach + 1) * rows
    slots = adjacency.shape[1]
    quarter = HD // QUAD
    vmem = pltpu.VMEM
    dma = pltpu.SemaphoreType.DMA
    scratch = [
        pltpu.SMEM(timesteps.shape, jnp.int32),
        vmem(qk_gain.shape, F32),
        pltpu.SMEM(adjacency.shape, jnp.int32),
        pltpu.SMEM(neighbour_count.shape, jnp.int32),
        pltpu.SMEM(anchor.shape, jnp.int32),
        vmem((rows, width), BF16),
        vmem((6 * local_w, freq), BF16),
        vmem((cols, width), BF16),
        vmem((cols, width), BF16),
        vmem((cols, width), BF16),
        vmem((width, ff), BF16),
        vmem((ff, width), BF16),
        vmem((rows, width), F32),
        vmem((rows, width), BF16),
        vmem((n_head, 8, 3 * local_w), BF16),
        vmem((3, 8, width), F32),
        vmem((rows, cols), BF16),
        vmem((view_count, HD, cols), BF16),
        vmem((cand_rows // HD, HD, cols), BF16),
        vmem((view_count, (slots + 2) * HD, cols), BF16),
        vmem((HD, cols), BF16),
        vmem((QUAD, quarter, cols), BF16),
        vmem((n_z, quarter, cols), BF16),
        vmem((quarter, cols), BF16),
        vmem((quarter, cols), BF16),
        vmem((HD, cols), BF16),
        vmem((rows, cols), BF16),
        vmem((rows, width), BF16),
        vmem((n_head, CHUNKS, blk, width), BF16),
        vmem((CHUNKS, blk, width), F32),
        vmem((CHUNKS, n_head * blk, width), BF16),
        vmem((rows, ff), BF16),
        vmem((rows, width), BF16),
        vmem((n_head, CHUNKS, blk, width), BF16),
        vmem((CHUNKS, blk, width), BF16),
        dma((21,)),
        dma((n_head,)),
        dma((n_head,)),
        dma((4, view_count)),
        dma((4, view_count)),
        dma((QUAD,)),
        dma((QUAD,)),
        dma((n_z,)),
        dma((n_z,)),
        dma((QUAD,)),
        dma((QUAD,)),
    ] + [dma((n_head, CHUNKS))] * 8
    return pl.pallas_call(
        functools.partial(kernel, n_view),
        out_shape=jax.ShapeDtypeStruct((rows, width), BF16),
        in_specs=[pl.BlockSpec(memory_space=pl.ANY)] * 11,
        out_specs=pl.BlockSpec(memory_space=pltpu.VMEM),
        scratch_shapes=scratch,
        compiler_params=pltpu.CompilerParams(
            collective_id=0, has_side_effects=True, vmem_limit_bytes=67043328
        ),
        name="layer",
    )(
        timesteps,
        qk_gain,
        adjacency,
        neighbour_count,
        anchor,
        tokens,
        modw,
        qkvw,
        out_weight,
        up_weight,
        down_weight,
    )


def solution(mesh):
    return jax.shard_map(
        functools.partial(body, mesh.shape["view"]),
        mesh=mesh,
        in_specs=(
            P("view", None),
            P("view"),
            P("view", None),
            P("view"),
            P(),
            P(None, None, "head"),
            P(None, None, "head"),
            P(None, "head"),
            P("head", None),
            P(None, "head"),
            P("head", None),
        ),
        out_specs=P("view", None),
        check_vma=False,
    )
```

```python
import functools
import math

import jax
import jax.numpy as jnp
from jax import lax
from jax.experimental import pallas as pl
from jax.experimental.pallas import tpu as pltpu
from jax.sharding import PartitionSpec as P

HD = 64
RADIUS = 8
EPSILON = 1e-06
MESH = pl.DeviceIdType.MESH
F32 = jnp.float32
BF16 = jnp.bfloat16

HEADS_X = 4
HEADS_Y = 2
QUAD = 4
CHUNKS = 2

DELTAS = [(2, 1), (1, 1), (3, 1), (2, 0), (0, 1), (1, 0), (3, 0)]
SPREAD = [(0, 1), (2, 0), (1, 0), (3, 0)]
FORWARDS = [((0, 1), [(1, 0), (3, 0)]), ((2, 0), [(0, 1)])]
RELAYED = [(4, (2, 1), (0, 1)), (2, (1, 1), (1, 0)), (3, (3, 1), (3, 0))]
DIRECT = [(0, (1, 0), (1, 0)), (1, (3, 0), (3, 0))]
MIXED = [(6, (2, 0), (4,)), (5, (0, 1), (2, 3))]
FINAL = [0, 1, 6, 5]
LAG = 0.2


def cos_sin(angle):
    turns = jnp.floor(angle * (2.0 / math.pi) + 0.5)
    r = angle - turns * 1.5703125
    r = r - turns * 4.837512969970703125e-4
    r = r - turns * 7.54978995489188216e-8
    s = r * r
    sin = r + r * s * (-1.6666654611e-1 + s * (8.3321608736e-3 - s * 1.9515295891e-4))
    cos = 1.0 - 0.5 * s + s * s * (4.166664568298827e-2 + s * (-1.388731625493765e-3 + s * 2.443315711809948e-5))
    part = turns - 4.0 * jnp.floor(turns * 0.25)
    odd = (part == 1.0) | (part == 3.0)
    base_c = jnp.where(odd, sin, cos)
    base_s = jnp.where(odd, cos, sin)
    return (
        jnp.where((part == 1.0) | (part == 2.0), -base_c, base_c),
        jnp.where((part == 2.0) | (part == 3.0), -base_s, base_s),
    )


def dot_nt(a, b):
    return lax.dot_general(a, b, (((1,), (1,)), ((), ())), preferred_element_type=F32)


def dot_nn(a, b):
    return lax.dot_general(a, b, (((1,), (0,)), ((), ())), preferred_element_type=F32)


def layer_norm(values):
    centre = values - jnp.mean(values, axis=-1, keepdims=True)
    return centre * lax.rsqrt(jnp.mean(centre * centre, axis=-1, keepdims=True) + EPSILON)


def kernel(
    n_view,
    ts_hbm,
    gain_hbm,
    adj_hbm,
    cnt_hbm,
    anc_hbm,
    tok_hbm,
    modw_hbm,
    qkvw_hbm,
    outw_hbm,
    upw_hbm,
    downw_hbm,
    out_ref,
    ts_ref,
    gain_ref,
    adj_ref,
    cnt_ref,
    anc_ref,
    tok,
    modw,
    wq,
    wkv,
    outw,
    upw,
    downw,
    normed,
    h1,
    modbuf,
    mods,
    qs,
    kv_own,
    cand,
    kvg,
    anc_src,
    anc_a,
    anc_b,
    anc_bsrc,
    anc_csrc,
    anc_full,
    att,
    part,
    rs,
    mix,
    resid,
    h2,
    hidden,
    part2,
    fin,
    ld_sem,
    mod_s,
    mod_r,
    kv_s,
    kv_r,
    aa_s,
    aa_r,
    ab_s,
    ab_r,
    ac_s,
    ac_r,
    ag1_s,
    ag1_r,
    rs_s,
    rs_r,
    ag2_s,
    ag2_r,
):
    v = lax.axis_index("view")
    h = lax.axis_index("head")
    xx, yh = h // HEADS_Y, h % HEADS_Y
    z, q = v // QUAD, v % QUAD
    n_z = n_view // QUAD
    n_head = HEADS_X * HEADS_Y
    width = tok.shape[1]
    rows = tok.shape[0]

    def head_peer(dx, dy):
        return ((xx + dx) % HEADS_X) * HEADS_Y + (yh + dy) % HEADS_Y

    def head_dev(dx, dy):
        return (v, head_peer(dx, dy))

    def view_dev(d):
        return ((v + d + n_view) % n_view, h)

    def quad_dev(dq):
        return (z * QUAD + (q + dq) % QUAD, h)

    def z_dev(dz):
        return (((z + dz) % n_z) * QUAD + q, h)

    def rcopy(src, dst, ss, rs, dev):
        return pltpu.make_async_remote_copy(
            src_ref=src, dst_ref=dst, send_sem=ss, recv_sem=rs, device_id=dev, device_id_type=MESH
        )

    barrier = pltpu.get_barrier_semaphore()
    partners = [head_dev(dx, dy) for dx, dy in DELTAS]
    partners += [view_dev(d) for d in (1, -1, 2, -2)]
    partners += [quad_dev(dq) for dq in range(1, QUAD)]
    partners += [z_dev(dz) for dz in range(1, n_z)]
    for dev in partners:
        pl.semaphore_signal(barrier, inc=1, device_id=dev, device_id_type=MESH)

    ld_ts = pltpu.make_async_copy(ts_hbm, ts_ref, ld_sem.at[16])
    ld_ts.start()
    ld_mod = pltpu.make_async_copy(modw_hbm, modw, ld_sem.at[0])
    ld_mod.start()
    ld_tok = pltpu.make_async_copy(tok_hbm, tok, ld_sem.at[1])
    ld_tok.start()
    ld_small = []
    for i, (src, dst) in enumerate(((gain_hbm, gain_ref), (adj_hbm, adj_ref), (cnt_hbm, cnt_ref), (anc_hbm, anc_ref))):
        c = pltpu.make_async_copy(src, dst, ld_sem.at[17 + i])
        c.start()
        ld_small.append(c)
    zero = jnp.zeros((HD, width), BF16)
    ld_qkv = []
    for i in range(3):
        wq[2 * i * HD + HD : 2 * i * HD + 2 * HD, :] = zero
        outw[2 * i * HD : 2 * i * HD + HD, :] = zero
        for s, (dst, at) in enumerate(
            ((wq, 2 * i * HD), (wkv, 2 * i * HD), (wkv, 2 * i * HD + HD))
        ):
            c = pltpu.make_async_copy(
                qkvw_hbm.at[s, pl.ds(i * HD, HD), :], dst.at[pl.ds(at, HD), :], ld_sem.at[2 + 3 * i + s]
            )
            c.start()
            ld_qkv.append(c)
    ld_out = []
    for i in range(3):
        c = pltpu.make_async_copy(
            outw_hbm.at[pl.ds(i * HD, HD), :], outw.at[pl.ds(2 * i * HD + HD, HD), :], ld_sem.at[11 + i]
        )
        c.start()
        ld_out.append(c)
    ld_up = pltpu.make_async_copy(upw_hbm, upw, ld_sem.at[14])
    ld_up.start()
    ld_down = pltpu.make_async_copy(downw_hbm, downw, ld_sem.at[15])
    ld_down.start()

    views = rows // HD
    ld_ts.wait()
    half_freq = modw.shape[1] // 2
    row8 = lax.broadcasted_iota(jnp.int32, (8, half_freq), 0)
    times = jnp.zeros((8, half_freq), jnp.int32)
    for j in range(views):
        times = jnp.where((row8 == j) | (row8 == j + 4), ts_ref[j], times)
    steps = lax.broadcasted_iota(jnp.int32, (8, half_freq), 1).astype(F32)
    cos, sin = cos_sin(times.astype(F32) * jnp.exp(steps * (-math.log(10000.0) / half_freq)))
    feats = jnp.concatenate([cos, sin], axis=1)
    act = (feats / (1.0 + jnp.exp(-feats))).astype(BF16)
    ld_mod.wait()
    local_w = modw.shape[0] // 6
    first = dot_nt(act, modw[0 : 3 * local_w, :])
    second = dot_nt(act, modw[3 * local_w : 6 * local_w, :])
    row8w = lax.broadcasted_iota(jnp.int32, first.shape, 0)
    modbuf[h] = jnp.where(row8w < 4, first, second).astype(BF16)
    pl.semaphore_wait(barrier, len(partners))
    mod_cps = []
    for dx, dy in DELTAS:
        k = dx * HEADS_Y + dy
        c = rcopy(modbuf.at[h], modbuf.at[h], mod_s.at[k], mod_r.at[k], head_dev(dx, dy))
        c.start()
        mod_cps.append(c)

    ld_tok.wait()
    step = 32
    for i in range(rows // step):
        at = slice(i * step, (i + 1) * step)
        normed[at, :] = layer_norm(tok[at, :].astype(F32))

    for c in mod_cps:
        c.wait_recv()
    for p in range(n_head):
        got = modbuf[p].astype(F32)
        for s in range(3):
            mods[s, :, p * local_w : (p + 1) * local_w] = got[:, s * local_w : (s + 1) * local_w]

    for j in range(views):
        shift = mods[0, j : j + 1, :]
        scale = 1.0 + mods[1, j : j + 1, :]
        at = slice(j * HD, (j + 1) * HD)
        h1[at, :] = (normed[at, :] * scale + shift).astype(BF16)

    for c in ld_qkv + ld_small:
        c.wait()
    lane = lax.broadcasted_iota(jnp.int32, (rows, 2 * HD), 1)
    low = lane < HD
    base = (RADIUS // views) * views
    for i in range(3):
        at = slice(2 * i * HD, 2 * (i + 1) * HD)
        kv = dot_nt(h1[...], wkv[at, :])
        gk = jnp.concatenate([gain_ref[1:2, i * HD : (i + 1) * HD], jnp.ones((1, HD), F32)], axis=1)
        ms = jnp.sum(jnp.where(low, kv * kv, 0.0), axis=-1, keepdims=True) * (1.0 / HD)
        kv = kv * jnp.where(low, lax.rsqrt(ms + EPSILON) * gk, 1.0)
        kvb = kv.astype(BF16)
        for j in range(views):
            kv_own[j, :, at] = kvb[j * HD : (j + 1) * HD, :]
            cand[base + j, :, at] = kvb[j * HD : (j + 1) * HD, :]

    core = v % 2
    mate = view_dev(1 - 2 * core)
    kv_cps = []
    fwd_cps = []

    def send_kv(j):
        for i, (dst, dev) in enumerate(
            (
                (base - 2 * views + j, view_dev(2)),
                (base + 2 * views + j, view_dev(-2)),
                (base - views + 2 * views * core + j, mate),
            )
        ):
            c = rcopy(kv_own.at[j], cand.at[dst], kv_s.at[i, j], kv_r.at[i, j], dev)
            c.start()
            kv_cps.append(c)

    def forward_kv(j):
        got = base + 2 * views - 4 * views * core + j
        rcopy(kv_own.at[j], cand.at[got], kv_s.at[0, j], kv_r.at[1 - core, j], mate).wait_recv()
        c = rcopy(
            cand.at[got], cand.at[base + views - 2 * views * core + j], kv_s.at[3, j], kv_r.at[3, j], mate
        )
        c.start()
        fwd_cps.append(c)

    anchor = anc_ref[0]
    piece = kv_own[lax.rem(anchor, views)]
    owners = jnp.zeros(piece.shape, jnp.int32) + lax.div(anchor, views)
    anc_src[...] = jnp.where(owners == v, piece.astype(F32), 0.0).astype(BF16)
    part_rows = HD // QUAD

    def quarter(ref, index):
        return ref.at[pl.ds(pl.multiple_of(index * part_rows, part_rows), part_rows), :]

    a_cps = []
    for dq in (2, 3, 1):
        peer = (q + dq) % QUAD
        c = rcopy(quarter(anc_src, peer), anc_a.at[dq], aa_s.at[dq], aa_r.at[dq], quad_dev(dq))
        c.start()
        a_cps.append(c)
    send_kv(0)
    send_kv(1)

    for i in range(3):
        at = slice(2 * i * HD, 2 * (i + 1) * HD)
        qq = dot_nt(h1[...], wq[at, :])
        gq = gain_ref[0:1, i * HD : (i + 1) * HD] * (1.0 / math.sqrt(HD))
        gq = jnp.concatenate([gq, jnp.zeros((1, HD), F32)], axis=1)
        ms = jnp.sum(qq * qq, axis=-1, keepdims=True) * (1.0 / HD)
        qs[:, at] = (qq * (lax.rsqrt(ms + EPSILON) * gq)).astype(BF16)

    for c in a_cps:
        c.wait_recv()
    mine_q = anc_src[pl.ds(pl.multiple_of(q * part_rows, part_rows), part_rows), :]
    anc_bsrc[...] = mine_q + anc_a[1] + anc_a[2] + anc_a[3]
    b_cps = []
    for dz in sorted(range(1, n_z), key=lambda d: -min(d, n_z - d)):
        c = rcopy(anc_bsrc, anc_b.at[dz], ab_s.at[dz], ab_r.at[dz], z_dev(dz))
        c.start()
        b_cps.append(c)
    for j in range(2, views):
        send_kv(j)
    forward_kv(0)
    forward_kv(1)
    for c in b_cps:
        c.wait_recv()
    total = anc_bsrc[...]
    for dz in range(1, n_z):
        total = total + anc_b[dz]
    anc_csrc[...] = total
    anc_full[pl.ds(pl.multiple_of(q * part_rows, part_rows), part_rows), :] = total
    c_cps = []
    for dq in (2, 3, 1):
        c = rcopy(anc_csrc, quarter(anc_full, q), ac_s.at[dq], ac_r.at[dq], quad_dev(dq))
        c.start()
        c_cps.append(c)
    for j in range(2, views):
        forward_kv(j)
    for j in range(views):
        got = base - 2 * views + 4 * views * core + j
        rcopy(kv_own.at[j], cand.at[got], kv_s.at[0, j], kv_r.at[core, j], mate).wait_recv()
        kv_cps[3 * j + 2].wait_recv()
        fwd_cps[j].wait_recv()
    for c in c_cps:
        c.wait_recv()

    full_views = n_view * views
    half = full_views // 2
    slots = adj_ref.shape[1]
    keys = (slots + 2) * HD
    cols = cand.shape[2]
    wlane = lax.broadcasted_iota(jnp.int32, (HD, cols), 1)
    klane = lax.broadcasted_iota(jnp.int32, (1, keys), 1)
    def attention(j):
        kvg[j, 0:HD, :] = kv_own[j]
        gid = v * views + j
        for s in range(slots):
            off = lax.rem(adj_ref[j, s] - gid + half + full_views, full_views) - half
            at = jnp.minimum(jnp.maximum(base + j + off, 0), cand.shape[0] - 1)
            kvg[j, (s + 1) * HD : (s + 2) * HD, :] = cand[at]
        kvg[j, (slots + 1) * HD : (slots + 2) * HD, :] = anc_full[...]
        qv = qs[j * HD : (j + 1) * HD, :]
        none = jnp.zeros_like(qv)
        qb = jnp.concatenate(
            [
                jnp.where((wlane >= 2 * i * HD) & (wlane < 2 * (i + 1) * HD), qv, none)
                for i in range(3)
            ],
            axis=0,
        )
        sc = dot_nt(qb, kvg[j])
        used = (klane < (cnt_ref[j] + 1) * HD) | (klane >= (slots + 1) * HD)
        sc = jnp.where(used, sc, -1e30)
        top = jnp.max(sc, axis=-1, keepdims=True)
        pw = jnp.exp(sc - top)
        den = jnp.sum(pw, axis=-1, keepdims=True)
        ov = dot_nn(pw.astype(BF16), kvg[j]) * (1.0 / den)
        res = jnp.zeros((HD, cols), F32)
        for i in range(3):
            keep = (wlane >= (2 * i + 1) * HD) & (wlane < 2 * (i + 1) * HD)
            res = jnp.where(keep, ov[i * HD : (i + 1) * HD, :], res)
        att[j * HD : (j + 1) * HD, :] = res.astype(BF16)

    tile = 256
    crows = rows // CHUNKS
    blk = crows // n_head
    ff = upw.shape[1]

    def rows_at(start, size):
        return pl.ds(pl.multiple_of(start, size), size)

    def mod_row(s, view):
        return mods[s % 3, pl.ds(view + 4 * (s // 3), 1), :]

    g1_cps, g2_cps = ([[] for _ in range(CHUNKS)] for _ in range(2))
    rs_cps = [[{} for _ in range(CHUNKS)] for _ in range(2)]

    def block_for(phase, c, dx, dy):
        if phase == 0:
            return part.at[rows_at(c * crows + head_peer(dx, dy) * blk, blk), :]
        k = (HEADS_X - dx) % HEADS_X * HEADS_Y + (HEADS_Y - dy) % HEADS_Y
        return part2.at[pl.ds(c * crows + k * blk, blk), :]

    def scatter(phase, c, slot, src, dx, dy):
        cp = rcopy(src, rs.at[phase, c, slot], rs_s.at[phase, c, slot], rs_r.at[phase, c, slot], head_dev(dx, dy))
        cp.start()
        rs_cps[phase][c][slot] = cp

    def scatter_first(phase, c):
        for slot, owner, hop in RELAYED + DIRECT:
            scatter(phase, c, slot, block_for(phase, c, *owner), *hop)

    def scatter_second(phase, c):
        for i, (slot, hop, parts) in enumerate(MIXED):
            total = block_for(phase, c, *hop)[...].astype(F32)
            for p in parts:
                rs_cps[phase][c][p].wait_recv()
                total = total + rs[phase, c, p].astype(F32)
            mix[phase, c, i] = total.astype(BF16)
            scatter(phase, c, slot, mix.at[phase, c, i], *hop)

    def scatter_sum(phase, c):
        total = block_for(phase, c, 0, 0)[...].astype(F32)
        for slot in FINAL:
            rs_cps[phase][c][slot].wait_recv()
            total = total + rs[phase, c, slot].astype(F32)
        return total

    def project(c):
        for j in range(c * crows // HD, (c + 1) * crows // HD):
            attention(j)
        span = slice(c * crows, (c + 1) * crows)
        for n in range(width // tile):
            at = slice(n * tile, (n + 1) * tile)
            part[span, at] = dot_nn(att[span, :], outw[:, at]).astype(BF16)
        scatter_first(0, c)

    def second_norm(c):
        mine = rows_at(c * crows + h * blk, blk)
        view = (c * crows + h * blk) // HD
        total = scatter_sum(0, c)
        res = tok[mine, :].astype(F32) + mod_row(2, view) * total
        resid[c] = res
        h2[c, 0:blk, :] = (layer_norm(res) * (1.0 + mod_row(4, view)) + mod_row(3, view)).astype(BF16)
        for dx, dy in SPREAD:
            g1_cps[c].append(gather1(c, (0, 0), dx, dy))

    def gather1(c, got, dx, dy):
        held = got[0] * HEADS_Y + got[1]
        k = (got[0] + dx) % HEADS_X * HEADS_Y + (got[1] + dy) % HEADS_Y
        src, dst = h2.at[c, pl.ds(held * blk, blk), :], h2.at[c, pl.ds(k * blk, blk), :]
        cp = rcopy(src, dst, ag1_s.at[k, c], ag1_r.at[k, c], head_dev(dx, dy))
        cp.start()
        return cp

    def gather2(c, got, dx, dy):
        k = (got[0] + dx) % HEADS_X * HEADS_Y + (got[1] + dy) % HEADS_Y
        owner = head_peer(HEADS_X - got[0], HEADS_Y - got[1])
        there = out_ref.at[rows_at(c * crows + owner * blk, blk), :]
        src = fin.at[c] if got == (0, 0) else there
        cp = rcopy(src, there, ag2_s.at[k, c], ag2_r.at[k, c], head_dev(dx, dy))
        cp.start()
        return cp

    def forward(gather, cps, c):
        for got, hops in FORWARDS:
            cps[c][SPREAD.index(got)].wait_recv()
            for dx, dy in hops:
                cps[c].append(gather(c, got, dx, dy))

    def arrived(cps, c):
        for i, cp in enumerate(cps[c]):
            if i >= len(SPREAD) or SPREAD[i] not in [got for got, _ in FORWARDS]:
                cp.wait_recv()

    def feed_forward(c):
        arrived(g1_cps, c)
        span = slice(c * crows, (c + 1) * crows)
        for n in range(ff // tile):
            at = slice(n * tile, (n + 1) * tile)
            u = dot_nn(h2[c], upw[:, at])
            hidden[span, at] = (
                0.5 * u * (1.0 + jnp.tanh(math.sqrt(2.0 / math.pi) * (u + 0.044715 * (u * u * u))))
            ).astype(BF16)
        for n in range(width // tile):
            at = slice(n * tile, (n + 1) * tile)
            part2[span, at] = dot_nn(hidden[span, :], downw[:, at]).astype(BF16)
        scatter_first(1, c)

    def finish(c):
        view = (c * crows + h * blk) // HD
        total = scatter_sum(1, c)
        done = (resid[c] + mod_row(5, view) * total).astype(BF16)
        fin[c] = done
        mine = rows_at(c * crows + h * blk, blk)
        out_ref[mine, :] = done
        for dx, dy in SPREAD:
            g2_cps[c].append(gather2(c, (0, 0), dx, dy))

    for c in ld_out + [ld_up, ld_down]:
        c.wait()
    stages = [
        project,
        functools.partial(scatter_second, 0),
        second_norm,
        functools.partial(forward, gather1, g1_cps),
        feed_forward,
        functools.partial(scatter_second, 1),
        finish,
        functools.partial(forward, gather2, g2_cps),
        functools.partial(arrived, g2_cps),
    ]
    order = sorted((i + LAG * c, c, i) for i in range(len(stages)) for c in range(CHUNKS))
    for _, c, i in order:
        stages[i](c)
    rest = [cp for phase in (g1_cps, g2_cps) for group in phase for cp in group]
    rest += [cp for phase in rs_cps for group in phase for cp in group.values()]
    for c in mod_cps + kv_cps + fwd_cps + a_cps + b_cps + c_cps + rest:
        c.wait_send()


def body(
    n_view,
    tokens,
    timesteps,
    adjacency,
    neighbour_count,
    anchor,
    mod_weight,
    qkv_weight,
    qk_gain,
    out_weight,
    up_weight,
    down_weight,
):
    view_count = timesteps.shape[0]
    rows, width = tokens.shape
    freq = mod_weight.shape[0]
    local_w = qkv_weight.shape[2]
    ff = up_weight.shape[1]
    cols = 2 * local_w
    modw = jnp.transpose(mod_weight, (1, 2, 0)).reshape(6 * local_w, freq)
    qkvw = jnp.transpose(qkv_weight, (1, 2, 0))
    n_head = HEADS_X * HEADS_Y
    blk = rows // n_head // CHUNKS
    n_z = n_view // QUAD
    reach = RADIUS // view_count
    cand_rows = (2 * reach + 1) * rows
    slots = adjacency.shape[1]
    quarter = HD // QUAD
    vmem = pltpu.VMEM
    dma = pltpu.SemaphoreType.DMA
    scratch = [
        pltpu.SMEM(timesteps.shape, jnp.int32),
        vmem(qk_gain.shape, F32),
        pltpu.SMEM(adjacency.shape, jnp.int32),
        pltpu.SMEM(neighbour_count.shape, jnp.int32),
        pltpu.SMEM(anchor.shape, jnp.int32),
        vmem((rows, width), BF16),
        vmem((6 * local_w, freq), BF16),
        vmem((cols, width), BF16),
        vmem((cols, width), BF16),
        vmem((cols, width), BF16),
        vmem((width, ff), BF16),
        vmem((ff, width), BF16),
        vmem((rows, width), F32),
        vmem((rows, width), BF16),
        vmem((n_head, 8, 3 * local_w), BF16),
        vmem((3, 8, width), F32),
        vmem((rows, cols), BF16),
        vmem((view_count, HD, cols), BF16),
        vmem((cand_rows // HD, HD, cols), BF16),
        vmem((view_count, (slots + 2) * HD, cols), BF16),
        vmem((HD, cols), BF16),
        vmem((QUAD, quarter, cols), BF16),
        vmem((n_z, quarter, cols), BF16),
        vmem((quarter, cols), BF16),
        vmem((quarter, cols), BF16),
        vmem((HD, cols), BF16),
        vmem((rows, cols), BF16),
        vmem((rows, width), BF16),
        vmem((2, CHUNKS, 7, blk, width), BF16),
        vmem((2, CHUNKS, 2, blk, width), BF16),
        vmem((CHUNKS, blk, width), F32),
        vmem((CHUNKS, n_head * blk, width), BF16),
        vmem((rows, ff), BF16),
        vmem((rows, width), BF16),
        vmem((CHUNKS, blk, width), BF16),
        dma((21,)),
        dma((n_head,)),
        dma((n_head,)),
        dma((4, view_count)),
        dma((4, view_count)),
        dma((QUAD,)),
        dma((QUAD,)),
        dma((n_z,)),
        dma((n_z,)),
        dma((QUAD,)),
        dma((QUAD,)),
    ] + [dma((n_head, CHUNKS))] * 2 + [dma((2, CHUNKS, 7))] * 2 + [dma((n_head, CHUNKS))] * 2
    return pl.pallas_call(
        functools.partial(kernel, n_view),
        out_shape=jax.ShapeDtypeStruct((rows, width), BF16),
        in_specs=[pl.BlockSpec(memory_space=pltpu.MemorySpace.HBM)] * 11,
        out_specs=pl.BlockSpec(memory_space=pltpu.VMEM),
        scratch_shapes=scratch,
        compiler_params=pltpu.CompilerParams(
            collective_id=0, has_side_effects=True, vmem_limit_bytes=64 * 1024 * 1024
        ),
        name="layer",
    )(
        timesteps,
        qk_gain,
        adjacency,
        neighbour_count,
        anchor,
        tokens,
        modw,
        qkvw,
        out_weight,
        up_weight,
        down_weight,
    )


def solution(mesh):
    return jax.shard_map(
        functools.partial(body, mesh.shape["view"]),
        mesh=mesh,
        in_specs=(
            P("view", None),
            P("view"),
            P("view", None),
            P("view"),
            P(),
            P(None, None, "head"),
            P(None, None, "head"),
            P(None, "head"),
            P("head", None),
            P(None, "head"),
            P("head", None),
        ),
        out_specs=P("view", None),
        check_vma=False,
    )
```

```python
import functools
import math

import jax
import jax.numpy as jnp
from jax import lax
from jax.experimental import pallas as pl
from jax.experimental.pallas import tpu as pltpu
from jax.sharding import PartitionSpec as P

HD = 64
RADIUS = 8
EPSILON = 1e-06
MESH = pl.DeviceIdType.MESH
F32 = jnp.float32
BF16 = jnp.bfloat16

HEADS_X = 4
HEADS_Y = 2
QUAD = 4
CHUNKS = 2

DELTAS = [(2, 1), (1, 1), (3, 1), (2, 0), (0, 1), (1, 0), (3, 0)]
SPREAD = [(0, 1), (2, 0), (1, 0), (3, 0)]
FORWARDS = [((2, 0), [(0, 1)]), ((0, 1), [(1, 0), (3, 0)])]
RELAYED = [(4, (2, 1), (0, 1)), (2, (1, 1), (1, 0)), (3, (3, 1), (3, 0))]
DIRECT = [(0, (1, 0), (1, 0)), (1, (3, 0), (3, 0))]
MIXED = [(5, (0, 1), (2, 3)), (6, (2, 0), (4,))]
FINAL = [0, 1, 6, 5]
LAG = 0.2


def cos_sin(angle):
    turns = jnp.floor(angle * (2.0 / math.pi) + 0.5)
    r = angle - turns * 1.5703125
    r = r - turns * 4.837512969970703125e-4
    r = r - turns * 7.54978995489188216e-8
    s = r * r
    sin = r + r * s * (-1.6666654611e-1 + s * (8.3321608736e-3 - s * 1.9515295891e-4))
    cos = 1.0 - 0.5 * s + s * s * (4.166664568298827e-2 + s * (-1.388731625493765e-3 + s * 2.443315711809948e-5))
    part = turns - 4.0 * jnp.floor(turns * 0.25)
    odd = (part == 1.0) | (part == 3.0)
    base_c = jnp.where(odd, sin, cos)
    base_s = jnp.where(odd, cos, sin)
    return (
        jnp.where((part == 1.0) | (part == 2.0), -base_c, base_c),
        jnp.where((part == 2.0) | (part == 3.0), -base_s, base_s),
    )


def dot_nt(a, b):
    return lax.dot_general(a, b, (((1,), (1,)), ((), ())), preferred_element_type=F32)


def dot_nn(a, b):
    return lax.dot_general(a, b, (((1,), (0,)), ((), ())), preferred_element_type=F32)


def layer_norm(values):
    centre = values - jnp.mean(values, axis=-1, keepdims=True)
    return centre * lax.rsqrt(jnp.mean(centre * centre, axis=-1, keepdims=True) + EPSILON)


def kernel(
    n_view,
    ts_hbm,
    gain_hbm,
    adj_hbm,
    cnt_hbm,
    anc_hbm,
    tok_hbm,
    modw_hbm,
    qkvw_hbm,
    outw_hbm,
    upw_hbm,
    downw_hbm,
    out_ref,
    ts_ref,
    gain_ref,
    adj_ref,
    cnt_ref,
    anc_ref,
    tok,
    modw,
    wq,
    wkv,
    outw,
    upw,
    downw,
    normed,
    h1,
    modbuf,
    mods,
    qs,
    kv_own,
    cand,
    kvg,
    anc_src,
    anc_a,
    anc_b,
    anc_bsrc,
    anc_csrc,
    anc_full,
    att,
    part,
    rs,
    mix,
    resid,
    h2,
    hidden,
    part2,
    fin,
    ld_sem,
    mod_s,
    mod_r,
    kv_s,
    kv_r,
    aa_s,
    aa_r,
    ab_s,
    ab_r,
    ac_s,
    ac_r,
    ag1_s,
    ag1_r,
    rs_s,
    rs_r,
    ag2_s,
    ag2_r,
):
    v = lax.axis_index("view")
    h = lax.axis_index("head")
    xx, yh = h // HEADS_Y, h % HEADS_Y
    z, q = v // QUAD, v % QUAD
    n_z = n_view // QUAD
    n_head = HEADS_X * HEADS_Y
    width = tok.shape[1]
    rows = tok.shape[0]

    def head_peer(dx, dy):
        return ((xx + dx) % HEADS_X) * HEADS_Y + (yh + dy) % HEADS_Y

    def head_dev(dx, dy):
        return (v, head_peer(dx, dy))

    def view_dev(d):
        return ((v + d + n_view) % n_view, h)

    def quad_dev(dq):
        return (z * QUAD + (q + dq) % QUAD, h)

    def z_dev(dz):
        return (((z + dz) % n_z) * QUAD + q, h)

    def rcopy(src, dst, ss, rs, dev):
        return pltpu.make_async_remote_copy(
            src_ref=src, dst_ref=dst, send_sem=ss, recv_sem=rs, device_id=dev, device_id_type=MESH
        )

    barrier = pltpu.get_barrier_semaphore()
    partners = [head_dev(dx, dy) for dx, dy in DELTAS]
    partners += [view_dev(d) for d in (1, -1, 2, -2)]
    partners += [quad_dev(dq) for dq in range(1, QUAD)]
    partners += [z_dev(dz) for dz in range(1, n_z)]
    for dev in partners:
        pl.semaphore_signal(barrier, inc=1, device_id=dev, device_id_type=MESH)

    ld_ts = pltpu.make_async_copy(ts_hbm, ts_ref, ld_sem.at[16])
    ld_ts.start()
    ld_mod = pltpu.make_async_copy(modw_hbm, modw, ld_sem.at[0])
    ld_mod.start()
    ld_tok = pltpu.make_async_copy(tok_hbm, tok, ld_sem.at[1])
    ld_tok.start()
    ld_small = []
    for i, (src, dst) in enumerate(((gain_hbm, gain_ref), (adj_hbm, adj_ref), (cnt_hbm, cnt_ref), (anc_hbm, anc_ref))):
        c = pltpu.make_async_copy(src, dst, ld_sem.at[17 + i])
        c.start()
        ld_small.append(c)
    zero = jnp.zeros((HD, width), BF16)
    ld_qkv = []
    for i in range(3):
        wq[2 * i * HD + HD : 2 * i * HD + 2 * HD, :] = zero
        outw[2 * i * HD : 2 * i * HD + HD, :] = zero
        for s, (dst, at) in enumerate(
            ((wq, 2 * i * HD), (wkv, 2 * i * HD), (wkv, 2 * i * HD + HD))
        ):
            c = pltpu.make_async_copy(
                qkvw_hbm.at[s, pl.ds(i * HD, HD), :], dst.at[pl.ds(at, HD), :], ld_sem.at[2 + 3 * i + s]
            )
            c.start()
            ld_qkv.append(c)
    ld_out = []
    for i in range(3):
        c = pltpu.make_async_copy(
            outw_hbm.at[pl.ds(i * HD, HD), :], outw.at[pl.ds(2 * i * HD + HD, HD), :], ld_sem.at[11 + i]
        )
        c.start()
        ld_out.append(c)
    ld_up = pltpu.make_async_copy(upw_hbm, upw, ld_sem.at[14])
    ld_up.start()
    ld_down = pltpu.make_async_copy(downw_hbm, downw, ld_sem.at[15])
    ld_down.start()

    views = rows // HD
    ld_ts.wait()
    half_freq = modw.shape[1] // 2
    row8 = lax.broadcasted_iota(jnp.int32, (8, half_freq), 0)
    times = jnp.zeros((8, half_freq), jnp.int32)
    for j in range(views):
        times = jnp.where((row8 == j) | (row8 == j + 4), ts_ref[j], times)
    steps = lax.broadcasted_iota(jnp.int32, (8, half_freq), 1).astype(F32)
    cos, sin = cos_sin(times.astype(F32) * jnp.exp(steps * (-math.log(10000.0) / half_freq)))
    feats = jnp.concatenate([cos, sin], axis=1)
    act = (feats / (1.0 + jnp.exp(-feats))).astype(BF16)
    ld_mod.wait()
    local_w = modw.shape[0] // 6
    first = dot_nt(act, modw[0 : 3 * local_w, :])
    second = dot_nt(act, modw[3 * local_w : 6 * local_w, :])
    row8w = lax.broadcasted_iota(jnp.int32, first.shape, 0)
    modbuf[h] = jnp.where(row8w < 4, first, second).astype(BF16)
    pl.semaphore_wait(barrier, len(partners))
    mod_cps = []
    for dx, dy in DELTAS:
        k = dx * HEADS_Y + dy
        c = rcopy(modbuf.at[h], modbuf.at[h], mod_s.at[k], mod_r.at[k], head_dev(dx, dy))
        c.start()
        mod_cps.append(c)

    ld_tok.wait()
    step = 32
    for i in range(rows // step):
        at = slice(i * step, (i + 1) * step)
        normed[at, :] = layer_norm(tok[at, :].astype(F32))

    for c in mod_cps:
        c.wait_recv()
    for p in range(n_head):
        got = modbuf[p].astype(F32)
        for s in range(3):
            mods[s, :, p * local_w : (p + 1) * local_w] = got[:, s * local_w : (s + 1) * local_w]

    for j in range(views):
        shift = mods[0, j : j + 1, :]
        scale = 1.0 + mods[1, j : j + 1, :]
        at = slice(j * HD, (j + 1) * HD)
        h1[at, :] = (normed[at, :] * scale + shift).astype(BF16)

    for c in ld_qkv + ld_small:
        c.wait()
    lane = lax.broadcasted_iota(jnp.int32, (rows, 2 * HD), 1)
    low = lane < HD
    base = (RADIUS // views) * views
    for i in range(3):
        at = slice(2 * i * HD, 2 * (i + 1) * HD)
        kv = dot_nt(h1[...], wkv[at, :])
        gk = jnp.concatenate([gain_ref[1:2, i * HD : (i + 1) * HD], jnp.ones((1, HD), F32)], axis=1)
        ms = jnp.sum(jnp.where(low, kv * kv, 0.0), axis=-1, keepdims=True) * (1.0 / HD)
        kv = kv * jnp.where(low, lax.rsqrt(ms + EPSILON) * gk, 1.0)
        kvb = kv.astype(BF16)
        for j in range(views):
            kv_own[j, :, at] = kvb[j * HD : (j + 1) * HD, :]
            cand[base + j, :, at] = kvb[j * HD : (j + 1) * HD, :]

    core = v % 2
    mate = view_dev(1 - 2 * core)
    kv_cps = []
    fwd_cps = []

    def send_kv(j):
        for i, (dst, dev) in enumerate(
            (
                (base - 2 * views + j, view_dev(2)),
                (base + 2 * views + j, view_dev(-2)),
                (base - views + 2 * views * core + j, mate),
            )
        ):
            c = rcopy(kv_own.at[j], cand.at[dst], kv_s.at[i, j], kv_r.at[i, j], dev)
            c.start()
            kv_cps.append(c)

    def forward_kv(j):
        got = base + 2 * views - 4 * views * core + j
        rcopy(kv_own.at[j], cand.at[got], kv_s.at[0, j], kv_r.at[1 - core, j], mate).wait_recv()
        c = rcopy(
            cand.at[got], cand.at[base + views - 2 * views * core + j], kv_s.at[3, j], kv_r.at[3, j], mate
        )
        c.start()
        fwd_cps.append(c)

    anchor = anc_ref[0]
    piece = kv_own[lax.rem(anchor, views)]
    owners = jnp.zeros(piece.shape, jnp.int32) + lax.div(anchor, views)
    anc_src[...] = jnp.where(owners == v, piece.astype(F32), 0.0).astype(BF16)
    part_rows = HD // QUAD

    def quarter(ref, index):
        return ref.at[pl.ds(pl.multiple_of(index * part_rows, part_rows), part_rows), :]

    a_cps = []
    for dq in (2, 3, 1):
        peer = (q + dq) % QUAD
        c = rcopy(quarter(anc_src, peer), anc_a.at[dq], aa_s.at[dq], aa_r.at[dq], quad_dev(dq))
        c.start()
        a_cps.append(c)
    send_kv(0)
    send_kv(1)

    for i in range(3):
        at = slice(2 * i * HD, 2 * (i + 1) * HD)
        qq = dot_nt(h1[...], wq[at, :])
        gq = gain_ref[0:1, i * HD : (i + 1) * HD] * (1.0 / math.sqrt(HD))
        gq = jnp.concatenate([gq, jnp.zeros((1, HD), F32)], axis=1)
        ms = jnp.sum(qq * qq, axis=-1, keepdims=True) * (1.0 / HD)
        qs[:, at] = (qq * (lax.rsqrt(ms + EPSILON) * gq)).astype(BF16)

    for c in a_cps:
        c.wait_recv()
    mine_q = anc_src[pl.ds(pl.multiple_of(q * part_rows, part_rows), part_rows), :]
    anc_bsrc[...] = mine_q + anc_a[1] + anc_a[2] + anc_a[3]
    b_cps = []
    for dz in sorted(range(1, n_z), key=lambda d: -min(d, n_z - d)):
        c = rcopy(anc_bsrc, anc_b.at[dz], ab_s.at[dz], ab_r.at[dz], z_dev(dz))
        c.start()
        b_cps.append(c)
    for j in range(2, views):
        send_kv(j)
    forward_kv(0)
    forward_kv(1)
    for c in b_cps:
        c.wait_recv()
    total = anc_bsrc[...]
    for dz in range(1, n_z):
        total = total + anc_b[dz]
    anc_csrc[...] = total
    anc_full[pl.ds(pl.multiple_of(q * part_rows, part_rows), part_rows), :] = total
    c_cps = []
    for dq in (2, 3, 1):
        c = rcopy(anc_csrc, quarter(anc_full, q), ac_s.at[dq], ac_r.at[dq], quad_dev(dq))
        c.start()
        c_cps.append(c)
    for j in range(2, views):
        forward_kv(j)
    for j in range(views):
        got = base - 2 * views + 4 * views * core + j
        rcopy(kv_own.at[j], cand.at[got], kv_s.at[0, j], kv_r.at[core, j], mate).wait_recv()
        kv_cps[3 * j + 2].wait_recv()
        fwd_cps[j].wait_recv()
    for c in c_cps:
        c.wait_recv()

    full_views = n_view * views
    half = full_views // 2
    slots = adj_ref.shape[1]
    keys = (slots + 2) * HD
    cols = cand.shape[2]
    wlane = lax.broadcasted_iota(jnp.int32, (HD, cols), 1)
    klane = lax.broadcasted_iota(jnp.int32, (1, keys), 1)
    def attention(j):
        kvg[j, 0:HD, :] = kv_own[j]
        gid = v * views + j
        for s in range(slots):
            off = lax.rem(adj_ref[j, s] - gid + half + full_views, full_views) - half
            at = jnp.minimum(jnp.maximum(base + j + off, 0), cand.shape[0] - 1)
            kvg[j, (s + 1) * HD : (s + 2) * HD, :] = cand[at]
        kvg[j, (slots + 1) * HD : (slots + 2) * HD, :] = anc_full[...]
        qv = qs[j * HD : (j + 1) * HD, :]
        none = jnp.zeros_like(qv)
        qb = jnp.concatenate(
            [
                jnp.where((wlane >= 2 * i * HD) & (wlane < 2 * (i + 1) * HD), qv, none)
                for i in range(3)
            ],
            axis=0,
        )
        sc = dot_nt(qb, kvg[j])
        used = (klane < (cnt_ref[j] + 1) * HD) | (klane >= (slots + 1) * HD)
        sc = jnp.where(used, sc, -1e30)
        top = jnp.max(sc, axis=-1, keepdims=True)
        pw = jnp.exp(sc - top)
        den = jnp.sum(pw, axis=-1, keepdims=True)
        ov = dot_nn(pw.astype(BF16), kvg[j]) * (1.0 / den)
        res = jnp.zeros((HD, cols), F32)
        for i in range(3):
            keep = (wlane >= (2 * i + 1) * HD) & (wlane < 2 * (i + 1) * HD)
            res = jnp.where(keep, ov[i * HD : (i + 1) * HD, :], res)
        att[j * HD : (j + 1) * HD, :] = res.astype(BF16)

    tile = 256
    crows = rows // CHUNKS
    blk = crows // n_head
    ff = upw.shape[1]

    def rows_at(start, size):
        return pl.ds(pl.multiple_of(start, size), size)

    def mod_row(s, view):
        return mods[s % 3, pl.ds(view + 4 * (s // 3), 1), :]

    g1_cps, g2_cps = ([[] for _ in range(CHUNKS)] for _ in range(2))
    rs_cps = [[{} for _ in range(CHUNKS)] for _ in range(2)]

    def block_for(phase, c, dx, dy):
        if phase == 0:
            return part.at[rows_at(c * crows + head_peer(dx, dy) * blk, blk), :]
        k = (HEADS_X - dx) % HEADS_X * HEADS_Y + (HEADS_Y - dy) % HEADS_Y
        return part2.at[pl.ds(c * crows + k * blk, blk), :]

    def scatter(phase, c, slot, src, dx, dy):
        cp = rcopy(src, rs.at[phase, c, slot], rs_s.at[phase, c, slot], rs_r.at[phase, c, slot], head_dev(dx, dy))
        cp.start()
        rs_cps[phase][c][slot] = cp

    def scatter_first(phase, c):
        for slot, owner, hop in RELAYED + DIRECT:
            scatter(phase, c, slot, block_for(phase, c, *owner), *hop)

    def scatter_second(phase, c):
        for i, (slot, hop, parts) in enumerate(MIXED):
            total = block_for(phase, c, *hop)[...].astype(F32)
            for p in parts:
                rs_cps[phase][c][p].wait_recv()
                total = total + rs[phase, c, p].astype(F32)
            mix[phase, c, i] = total.astype(BF16)
            scatter(phase, c, slot, mix.at[phase, c, i], *hop)

    def scatter_sum(phase, c):
        total = block_for(phase, c, 0, 0)[...].astype(F32)
        for slot in FINAL:
            rs_cps[phase][c][slot].wait_recv()
            total = total + rs[phase, c, slot].astype(F32)
        return total

    def project(c):
        for j in range(c * crows // HD, (c + 1) * crows // HD):
            attention(j)
        span = slice(c * crows, (c + 1) * crows)
        for n in range(width // tile):
            at = slice(n * tile, (n + 1) * tile)
            part[span, at] = dot_nn(att[span, :], outw[:, at]).astype(BF16)
        scatter_first(0, c)

    def second_norm(c):
        mine = rows_at(c * crows + h * blk, blk)
        view = (c * crows + h * blk) // HD
        total = scatter_sum(0, c)
        res = tok[mine, :].astype(F32) + mod_row(2, view) * total
        resid[c] = res
        h2[c, 0:blk, :] = (layer_norm(res) * (1.0 + mod_row(4, view)) + mod_row(3, view)).astype(BF16)
        for dx, dy in SPREAD:
            g1_cps[c].append(gather1(c, (0, 0), dx, dy))

    def gather1(c, got, dx, dy):
        held = got[0] * HEADS_Y + got[1]
        k = (got[0] + dx) % HEADS_X * HEADS_Y + (got[1] + dy) % HEADS_Y
        src, dst = h2.at[c, pl.ds(held * blk, blk), :], h2.at[c, pl.ds(k * blk, blk), :]
        cp = rcopy(src, dst, ag1_s.at[k, c], ag1_r.at[k, c], head_dev(dx, dy))
        cp.start()
        return cp

    def gather2(c, got, dx, dy):
        k = (got[0] + dx) % HEADS_X * HEADS_Y + (got[1] + dy) % HEADS_Y
        owner = head_peer(HEADS_X - got[0], HEADS_Y - got[1])
        there = out_ref.at[rows_at(c * crows + owner * blk, blk), :]
        src = fin.at[c] if got == (0, 0) else there
        cp = rcopy(src, there, ag2_s.at[k, c], ag2_r.at[k, c], head_dev(dx, dy))
        cp.start()
        return cp

    def forward(gather, cps, c):
        for got, hops in FORWARDS:
            cps[c][SPREAD.index(got)].wait_recv()
            for dx, dy in hops:
                cps[c].append(gather(c, got, dx, dy))

    def arrived(cps, c):
        for i, cp in enumerate(cps[c]):
            if i >= len(SPREAD) or SPREAD[i] not in [got for got, _ in FORWARDS]:
                cp.wait_recv()

    def feed_forward(c):
        arrived(g1_cps, c)
        span = slice(c * crows, (c + 1) * crows)
        for n in range(ff // tile):
            at = slice(n * tile, (n + 1) * tile)
            u = dot_nn(h2[c], upw[:, at])
            hidden[span, at] = (
                0.5 * u * (1.0 + jnp.tanh(math.sqrt(2.0 / math.pi) * (u + 0.044715 * (u * u * u))))
            ).astype(BF16)
        for n in range(width // tile):
            at = slice(n * tile, (n + 1) * tile)
            part2[span, at] = dot_nn(hidden[span, :], downw[:, at]).astype(BF16)
        scatter_first(1, c)

    def finish(c):
        view = (c * crows + h * blk) // HD
        total = scatter_sum(1, c)
        done = (resid[c] + mod_row(5, view) * total).astype(BF16)
        fin[c] = done
        mine = rows_at(c * crows + h * blk, blk)
        out_ref[mine, :] = done
        for dx, dy in SPREAD:
            g2_cps[c].append(gather2(c, (0, 0), dx, dy))

    for c in ld_out + [ld_up, ld_down]:
        c.wait()
    stages = [
        project,
        functools.partial(scatter_second, 0),
        second_norm,
        functools.partial(forward, gather1, g1_cps),
        feed_forward,
        functools.partial(scatter_second, 1),
        finish,
        functools.partial(forward, gather2, g2_cps),
        functools.partial(arrived, g2_cps),
    ]
    order = sorted((i + LAG * c, c, i) for i in range(len(stages)) for c in range(CHUNKS))
    for _, c, i in order:
        stages[i](c)
    rest = [cp for phase in (g1_cps, g2_cps) for group in phase for cp in group]
    rest += [cp for phase in rs_cps for group in phase for cp in group.values()]
    for c in mod_cps + kv_cps + fwd_cps + a_cps + b_cps + c_cps + rest:
        c.wait_send()


def in_hbm(operand):
    return pltpu.with_memory_space_constraint(operand, pltpu.MemorySpace.HBM)


def body(
    n_view,
    tokens,
    timesteps,
    adjacency,
    neighbour_count,
    anchor,
    mod_weight,
    qkv_weight,
    qk_gain,
    out_weight,
    up_weight,
    down_weight,
):
    view_count = timesteps.shape[0]
    rows, width = tokens.shape
    freq = mod_weight.shape[0]
    local_w = qkv_weight.shape[2]
    ff = up_weight.shape[1]
    cols = 2 * local_w
    modw = jnp.transpose(mod_weight, (1, 2, 0)).reshape(6 * local_w, freq)
    qkvw = jnp.transpose(qkv_weight, (1, 2, 0))
    n_head = HEADS_X * HEADS_Y
    blk = rows // n_head // CHUNKS
    n_z = n_view // QUAD
    reach = RADIUS // view_count
    cand_rows = (2 * reach + 1) * rows
    slots = adjacency.shape[1]
    quarter = HD // QUAD
    vmem = pltpu.VMEM
    dma = pltpu.SemaphoreType.DMA
    scratch = [
        pltpu.SMEM(timesteps.shape, jnp.int32),
        vmem(qk_gain.shape, F32),
        pltpu.SMEM(adjacency.shape, jnp.int32),
        pltpu.SMEM(neighbour_count.shape, jnp.int32),
        pltpu.SMEM(anchor.shape, jnp.int32),
        vmem((rows, width), BF16),
        vmem((6 * local_w, freq), BF16),
        vmem((cols, width), BF16),
        vmem((cols, width), BF16),
        vmem((cols, width), BF16),
        vmem((width, ff), BF16),
        vmem((ff, width), BF16),
        vmem((rows, width), F32),
        vmem((rows, width), BF16),
        vmem((n_head, 8, 3 * local_w), BF16),
        vmem((3, 8, width), F32),
        vmem((rows, cols), BF16),
        vmem((view_count, HD, cols), BF16),
        vmem((cand_rows // HD, HD, cols), BF16),
        vmem((view_count, (slots + 2) * HD, cols), BF16),
        vmem((HD, cols), BF16),
        vmem((QUAD, quarter, cols), BF16),
        vmem((n_z, quarter, cols), BF16),
        vmem((quarter, cols), BF16),
        vmem((quarter, cols), BF16),
        vmem((HD, cols), BF16),
        vmem((rows, cols), BF16),
        vmem((rows, width), BF16),
        vmem((2, CHUNKS, 7, blk, width), BF16),
        vmem((2, CHUNKS, 2, blk, width), BF16),
        vmem((CHUNKS, blk, width), F32),
        vmem((CHUNKS, n_head * blk, width), BF16),
        vmem((rows, ff), BF16),
        vmem((rows, width), BF16),
        vmem((CHUNKS, blk, width), BF16),
        dma((21,)),
        dma((n_head,)),
        dma((n_head,)),
        dma((4, view_count)),
        dma((4, view_count)),
        dma((QUAD,)),
        dma((QUAD,)),
        dma((n_z,)),
        dma((n_z,)),
        dma((QUAD,)),
        dma((QUAD,)),
    ] + [dma((n_head, CHUNKS))] * 2 + [dma((2, CHUNKS, 7))] * 2 + [dma((n_head, CHUNKS))] * 2
    return pl.pallas_call(
        functools.partial(kernel, n_view),
        out_shape=jax.ShapeDtypeStruct((rows, width), BF16),
        in_specs=[pl.BlockSpec(memory_space=pltpu.MemorySpace.HBM)] * 11,
        out_specs=pl.BlockSpec(memory_space=pltpu.VMEM),
        scratch_shapes=scratch,
        compiler_params=pltpu.CompilerParams(
            collective_id=0, has_side_effects=True, vmem_limit_bytes=48 * 1024 * 1024
        ),
        name="layer",
    )(
        in_hbm(timesteps),
        in_hbm(qk_gain),
        in_hbm(adjacency),
        in_hbm(neighbour_count),
        anchor,
        *(in_hbm(operand) for operand in (tokens, modw, qkvw, out_weight, up_weight, down_weight)),
    )


def solution(mesh):
    return jax.shard_map(
        functools.partial(body, mesh.shape["view"]),
        mesh=mesh,
        in_specs=(
            P("view", None),
            P("view"),
            P("view", None),
            P("view"),
            P(),
            P(None, None, "head"),
            P(None, None, "head"),
            P(None, "head"),
            P("head", None),
            P(None, "head"),
            P("head", None),
        ),
        out_specs=P("view", None),
        check_vma=False,
    )
```
